512 devices in a mesh: own: 64 (over x, z), pair: 8 (over y, core).
Axes of the slice: x: 4, y: 4, z: 16, core: 2. Of those that a mesh axis runs over, the one named last changes fastest.
Arguments:
- embeddings: float32 [128, 128, 1024], P('own'), as said below
- cluster_sizes: int32 [32], replicated, may hold values from 1 to 12, 128 in all
- row_counts: int32 [128], replicated, may hold values from 32 to 128, as said below
Outputs:
- near_sums: bfloat16 [128, 128, 1024], P('own', 'pair')
- log_masses: float32 [128, 128], P('own', 'pair')
The draws below stay inside these ranges and needn't reach their ends.
Inputs may be any that keep to these rules, and one draw needn't show every extreme that they name: `row_counts`: some block has all 128 valid rows. `embeddings`: finite rows of nonzero norm.
All inputs are finite; a program needn't handle non-finite values.
Results may differ from the reference program's by a relative error of at most 0.01.
Values may be sent and summed in bfloat16 or wider, within the bound.
No kernel may reach another device: no remote copies, remote signals or barrier semaphores. Data moves between devices by JAX's collectives and lax.ppermute only.
A program may use at most 64 MiB of HBM per device.

```python
import math
import jax
import jax.numpy as jnp
import numpy as np
from jax import lax

W = 1024
R = 128
SPAN = 12
BLOCKS = 128
CLUSTERS = 32


def draw_embeddings(key, part):
    subkeys = jax.random.split(key, 1)
    base_rows = jax.random.normal(subkeys[0], (BLOCKS, R, W), jnp.float32)
    return base_rows


def draw_row_counts(key, part):
    first_key, second_key = jax.random.split(key)
    counts = jax.random.randint(first_key, (BLOCKS,), max(2, R // 4), R + 1)
    full_block = jax.random.randint(second_key, (), 0, BLOCKS)
    return jnp.where(jnp.arange(BLOCKS) == full_block, R, counts).astype(jnp.int32)


def split_up(count, total, reach, lean):
    weights = [(1 << 20) // math.isqrt(standing ** lean) + 1 for standing in range(2, count + 1)]
    surplus, given = total - reach - (count - 1), [1] * (count - 1)
    while surplus > 0:
        candidates = [i for i in range(count - 1) if given[i] < reach]
        mass, remaining = sum([weights[i] for i in candidates]), surplus
        for i in candidates:
            extra = min(reach - given[i], max(1, remaining * weights[i] // mass), surplus)
            given[i] = given[i] + extra
            surplus = surplus - extra
    return np.array([reach] + given)


def ragged(rng, count, total, bound, slope):
    if count == 2:
        one = jax.random.randint(rng, (), max(1, total - bound), min(bound, total - 1) + 1)
        return jnp.stack([one, total - one])
    lengths = jnp.asarray(split_up(count, total, bound, slope), jnp.int32)
    couples = (count - 1) // 2
    donor, receiver = lengths[1:1 + 2 * couples:2], lengths[2:2 + 2 * couples:2]
    margin = jnp.minimum(donor - 1, bound - receiver)
    passed = jax.random.randint(jax.random.fold_in(rng, 1), (couples,), 0, 1 << 20) % (margin + 1)
    lengths = lengths.at[1:1 + 2 * couples:2].set(donor - passed).at[2:2 + 2 * couples:2].set(receiver + passed)
    return lengths[jax.random.permutation(jax.random.fold_in(rng, 2), count)]


def setup_inputs(seed: int = 0) -> dict:
    key_of = jax.random.split(jax.random.key(seed), 4)
    return {
        "embeddings": draw_embeddings(jax.random.fold_in(key_of[3], 71), 0),
        "cluster_sizes": ragged(key_of[1], CLUSTERS, BLOCKS, SPAN, 2).astype(jnp.int32),
        "row_counts": draw_row_counts(jax.random.fold_in(key_of[3], 71), 0),
    }


sharpness = 128.0
negative = -1e+30

def unit_rows(values):
    squares = lax.optimization_barrier(jnp.sum(values * values, axis=-1, keepdims=True))
    return (values * lax.rsqrt(squares + 1e-06)).astype(jnp.bfloat16)

def reference(embeddings, cluster_sizes, row_counts):
    normed = unit_rows(embeddings)
    cluster_start = jnp.cumsum(cluster_sizes) - cluster_sizes
    block_ids = jnp.arange(BLOCKS, dtype=jnp.int32)
    owner_cluster = lax.optimization_barrier(jnp.sum((block_ids[:, None] >= cluster_start[None, :]).astype(jnp.int32), axis=1)) - 1
    row_index = jnp.arange(R, dtype=jnp.int32)

    def one_block(block):
        queries = normed[block]

        def tile_step(carried, offset):
            source = block + offset
            inside = (source >= 0) & (source < BLOCKS)
            clipped = jnp.clip(source, 0, BLOCKS - 1).astype(jnp.int32)
            same_cluster = inside & (owner_cluster[clipped] == owner_cluster[block])

            def score_tile(running):
                run_max, run_mass, run_sum = running
                key_rows = normed[clipped]
                scores = sharpness * jnp.dot(queries, key_rows.T, preferred_element_type=jnp.float32)
                kept = (row_index[None, :] < row_counts[clipped]) & ((offset != 0) | (row_index[:, None] != row_index[None, :]))
                scores = jnp.where(kept, scores, negative)
                row_top = lax.optimization_barrier(jnp.max(scores, axis=1))
                weight = jnp.where(kept, jnp.exp(scores - row_top[:, None]), 0.0)
                partial_value = jnp.dot(weight.astype(jnp.bfloat16), key_rows, preferred_element_type=jnp.float32)
                new_max = jnp.maximum(run_max, row_top)
                old_scale = jnp.exp(run_max - new_max)
                new_scale = jnp.exp(row_top - new_max)
                return (new_max, run_mass * old_scale + lax.optimization_barrier(jnp.sum(weight, axis=1)) * new_scale, run_sum * old_scale[:, None] + partial_value * new_scale[:, None])
            return (lax.cond(same_cluster, score_tile, lambda running: running, carried), None)
        start_state = (jnp.full((R,), negative, jnp.float32), jnp.zeros((R,), jnp.float32), jnp.zeros((R, W), jnp.float32))
        offsets = jnp.arange(-(SPAN - 1), SPAN, dtype=jnp.int32)
        run_max, run_mass, run_sum = lax.scan(tile_step, start_state, offsets)[0]
        row_valid = row_index < row_counts[block]
        sums_here = jnp.where(row_valid[:, None], run_sum / run_mass[:, None], 0.0).astype(jnp.bfloat16)
        mass_here = jnp.where(row_valid, run_max + jnp.log(run_mass), 0.0)
        return (sums_here, mass_here)
    near_sums, log_masses = lax.map(one_block, block_ids)
    return (near_sums, log_masses)
```

```python
import jax
import jax.numpy as jnp
from jax import lax
from jax.experimental import pallas as pl
from jax.experimental.pallas import tpu as pltpu
from jax.sharding import PartitionSpec as P

SHARPNESS = 128.0
NEGATIVE = -1e30
REACH = 6
LANES = 128
AXES = ("own", "pair")


def handed_on(shard, by, own_count, pair_count):
    pairs = []
    for owner in range(own_count):
        for place in range(pair_count):
            target = owner + (by if place % 2 == 0 else -by)
            if 0 <= target < own_count:
                pairs.append((owner * pair_count + place, target * pair_count + place))
    return lax.ppermute(shard, AXES, pairs)


def unit_kernel(x_ref, normed_ref, part_ref):
    rows = x_ref.shape[0] // 2
    part = part_ref.shape[0] // 2
    for local in range(2):
        x = x_ref[local * rows : (local + 1) * rows, :]
        squares = jnp.sum(x * x, axis=1, keepdims=True)
        normed_ref[local * rows : (local + 1) * rows, :] = (x * lax.rsqrt(squares + 1e-06)).astype(
            jnp.bfloat16
        )
    place = lax.axis_index("pair")
    side = lax.rem(place, 2)
    start = (place // 2) * part
    for half in range(2):
        local = side if half else 1 - side
        part_ref[half * part : (half + 1) * part, :] = normed_ref[
            pl.ds(pl.multiple_of(local * rows + start, part), part), :
        ]


def unit_rows(values, part_rows):
    rows, features = values.shape
    return pl.pallas_call(
        unit_kernel,
        out_shape=(
            jax.ShapeDtypeStruct((rows, features), jnp.bfloat16),
            jax.ShapeDtypeStruct((part_rows, features), jnp.bfloat16),
        ),
        in_specs=[pl.BlockSpec(memory_space=pltpu.VMEM)],
        out_specs=(pl.BlockSpec(memory_space=pltpu.VMEM), pl.BlockSpec(memory_space=pltpu.VMEM)),
        compiler_params=pltpu.CompilerParams(vmem_limit_bytes=16 << 20),
        cost_estimate=pl.CostEstimate(
            flops=4 * rows * features, bytes_accessed=6 * rows * features, transcendentals=rows
        ),
        name="unit_rows",
    )(values)


def score_kernel(clusters_ref, key_ref, q_ref, part_ref, *refs):
    *shard_refs, out_ref, keys = refs
    step = part_ref.shape[0]
    keys[0:step, :] = part_ref[...]
    keys[step : 2 * step, :] = part_ref[...]
    for i, ref in enumerate(shard_refs):
        keys[(i + 2) * step : (i + 3) * step, :] = ref[...]
    features = q_ref.shape[1]
    rows = q_ref.shape[0] // 2
    pair_count = out_ref.shape[0]
    slice_rows = rows // pair_count
    first_row = lax.axis_index("own") * (2 * rows)
    key_cluster = key_ref[0:1, :]
    key_row = key_ref[1:2, :]
    for local in range(2):
        queries = q_ref[local * rows : (local + 1) * rows, :]
        scores = SHARPNESS * lax.dot_general(
            queries, keys[...], (((1,), (1,)), ((), ())), preferred_element_type=jnp.float32
        )
        row = first_row + local * rows + lax.broadcasted_iota(jnp.int32, (rows, 1), 0)
        kept = (key_cluster == clusters_ref[local]) & (key_row != row)
        scores = jnp.where(kept, scores, NEGATIVE)
        top = jnp.max(scores, axis=1, keepdims=True)
        weight = jnp.where(kept, jnp.exp(scores - top), 0.0)
        mass = jnp.sum(weight, axis=1, keepdims=True)
        some = mass > 0.0
        safe = jnp.where(some, mass, 1.0)
        total = jnp.dot(weight.astype(jnp.bfloat16), keys[...], preferred_element_type=jnp.float32)
        mean = (total / safe).astype(jnp.bfloat16)
        log_mass = jnp.where(some, top + jnp.log(safe), NEGATIVE)
        high = log_mass.astype(jnp.bfloat16).astype(jnp.float32)
        middle = (log_mass - high).astype(jnp.bfloat16).astype(jnp.float32)
        low = log_mass - high - middle
        lane = lax.broadcasted_iota(jnp.int32, (rows, LANES), 1)
        pieces = jnp.where(lane == 0, high, jnp.where(lane == 1, middle, low)).astype(jnp.bfloat16)
        for place in range(pair_count):
            here = slice(place * slice_rows, (place + 1) * slice_rows)
            there = slice(local * slice_rows, (local + 1) * slice_rows)
            out_ref[place, there, 0:features] = mean[here, :]
            out_ref[place, there, features : features + LANES] = pieces[here, :]


def partial_states(clusters, key_table, normed, part, shards, pair_count):
    rows, features = normed.shape
    step = part.shape[0]
    key_rows = step * (len(shards) + 2)
    vmem = pl.BlockSpec(memory_space=pltpu.VMEM)
    return pl.pallas_call(
        score_kernel,
        out_shape=jax.ShapeDtypeStruct(
            (pair_count, rows // pair_count, features + LANES), jnp.bfloat16
        ),
        in_specs=[pl.BlockSpec(memory_space=pltpu.SMEM)] + [vmem] * (3 + len(shards)),
        out_specs=vmem,
        scratch_shapes=[pltpu.VMEM((key_rows, features), jnp.bfloat16)],
        compiler_params=pltpu.CompilerParams(vmem_limit_bytes=24 << 20),
        cost_estimate=pl.CostEstimate(
            flops=4 * rows * key_rows * features,
            bytes_accessed=4 * (rows + key_rows) * features,
            transcendentals=rows * key_rows,
        ),
        name="partial_states",
    )(clusters, key_table, normed, part, *shards)


def merge_kernel(counts_ref, in_ref, near_ref, log_ref):
    pair_count, rows, wide = in_ref.shape
    features = wide - LANES
    slice_rows = rows // 2
    logs = []
    for i in range(pair_count):
        pieces = in_ref[i, :, features:wide].astype(jnp.float32)
        logs.append(pieces[:, 0:1] + pieces[:, 1:2] + pieces[:, 2:3])
    top = logs[0]
    for one in logs[1:]:
        top = jnp.maximum(top, one)
    scales = [jnp.exp(one - top) for one in logs]
    mass = scales[0]
    for one in scales[1:]:
        mass = mass + one
    total = scales[0] * in_ref[0, :, 0:features].astype(jnp.float32)
    for i in range(1, pair_count):
        total = total + scales[i] * in_ref[i, :, 0:features].astype(jnp.float32)
    near = total / mass
    log_mass = top + jnp.log(mass)
    first = lax.axis_index("pair") * slice_rows
    row = first + lax.broadcasted_iota(jnp.int32, (slice_rows, 1), 0)
    same = lax.broadcasted_iota(jnp.int32, (slice_rows, slice_rows), 0) == lax.broadcasted_iota(
        jnp.int32, (slice_rows, slice_rows), 1
    )
    for local in range(2):
        here = slice(local * slice_rows, (local + 1) * slice_rows)
        valid = row < counts_ref[local]
        near_ref[local] = jnp.where(valid, near[here, :], 0.0).astype(near_ref.dtype)
        column = jnp.where(valid, log_mass[here, :], 0.0)
        log_ref[local : local + 1, :] = jnp.sum(
            jnp.where(same, column, 0.0), axis=0, keepdims=True
        )


def merged(counts, arrived):
    pair_count, rows, wide = arrived.shape
    features = wide - LANES
    vmem = pl.BlockSpec(memory_space=pltpu.VMEM)
    return pl.pallas_call(
        merge_kernel,
        out_shape=(
            jax.ShapeDtypeStruct((2, rows // 2, features), jnp.bfloat16),
            jax.ShapeDtypeStruct((2, rows // 2), jnp.float32),
        ),
        in_specs=[pl.BlockSpec(memory_space=pltpu.SMEM), vmem],
        out_specs=(vmem, vmem),
        compiler_params=pltpu.CompilerParams(vmem_limit_bytes=16 << 20),
        cost_estimate=pl.CostEstimate(
            flops=4 * pair_count * rows * features,
            bytes_accessed=2 * (pair_count + 1) * rows * wide,
            transcendentals=pair_count * rows,
        ),
        name="merged",
    )(counts, arrived)


def body(embeddings, cluster_sizes, row_counts):
    local_blocks, block_rows, features = embeddings.shape
    own_count, pair_count = lax.axis_size("own"), lax.axis_size("pair")
    block_total = own_count * local_blocks
    own, place = lax.axis_index("own"), lax.axis_index("pair")
    side = place % 2
    part = block_rows // (pair_count // 2)
    step = local_blocks * part

    normed, own_part = unit_rows(embeddings.reshape(local_blocks * block_rows, features), step)
    shards = {by: handed_on(own_part, by, own_count, pair_count) for by in (3, 2, 1)}
    for by in (3, 2, 1):
        shards[3 + by] = handed_on(shards[3], by, own_count, pair_count)

    clusters = jnp.arange(cluster_sizes.shape[0], dtype=jnp.int32)
    cluster_start = jnp.sum(
        jnp.where(clusters[:, None] > clusters[None, :], cluster_sizes[None, :], 0), axis=1
    )

    def cluster_of(blocks):
        return jnp.sum((blocks[:, None] >= cluster_start[None, :]).astype(jnp.int32), axis=1) - 1

    def count_of(blocks):
        places = jnp.arange(block_total, dtype=jnp.int32)
        return jnp.sum(jnp.where(blocks[:, None] == places[None, :], row_counts[None, :], 0), axis=1)

    slots = jnp.arange(step * (REACH + 2), dtype=jnp.int32)
    group, within = slots // step, slots % step
    half, sub = within // part, within % part
    offset = jnp.maximum(group - 1, 0)
    key_owner = own + jnp.where(side == 0, -offset, offset)
    key_block = key_owner * local_blocks + jnp.where(half == 0, 1 - side, side)
    row_in_block = (place // 2) * part + sub
    mine = (group != 0) | (sub // (part // 2) == side)
    usable = (row_in_block < count_of(key_block)) & mine & (group != 1)
    key_cluster = jnp.where(usable, cluster_of(key_block), -1)
    key_table = jnp.stack([key_cluster, key_block * block_rows + row_in_block])
    own_blocks = own * local_blocks + jnp.arange(local_blocks, dtype=jnp.int32)

    states = partial_states(
        cluster_of(own_blocks),
        key_table,
        normed,
        own_part,
        [shards[by] for by in range(1, REACH + 1)],
        pair_count,
    )
    arrived = lax.all_to_all(states, "pair", split_axis=0, concat_axis=0, tiled=True)
    return merged(count_of(own_blocks), arrived)


def solution(mesh):
    placed = (P("own", None, None), P(), P())
    return jax.shard_map(
        body,
        mesh=mesh,
        in_specs=placed,
        out_specs=(P("own", "pair", None), P("own", "pair")),
        check_vma=False,
    )
```

```python
import jax
import jax.numpy as jnp
from jax import lax
from jax.experimental import pallas as pl
from jax.experimental.pallas import tpu as pltpu
from jax.sharding import PartitionSpec as P

SHARPNESS = 128.0
NEGATIVE = -1e30
REACH = 6
LANES = 128
AXES = ("own", "pair")


def handed_on(shard, by, own_count, pair_count):
    pairs = []
    for owner in range(own_count):
        for place in range(pair_count):
            target = owner + (by if place % 2 == 0 else -by)
            if 0 <= target < own_count:
                pairs.append((owner * pair_count + place, target * pair_count + place))
    return lax.ppermute(shard, AXES, pairs)


def unit_rows(values):
    squares = jnp.sum(values * values, axis=1, keepdims=True)
    return (values * lax.rsqrt(squares + 1e-06)).astype(jnp.bfloat16)


def part_kernel(x_ref, part_ref, rows, sems):
    part = rows.shape[1]
    place = lax.axis_index("pair")
    side = lax.rem(place, 2)
    start = pl.multiple_of(lax.shift_right_logical(place, 1) * part, part)
    copies = []
    for half in range(2):
        local = side if half else 1 - side
        copies.append(
            pltpu.make_async_copy(
                x_ref.at[local, pl.ds(start, part), :], rows.at[half], sems.at[half]
            )
        )
        copies[half].start()
    for half in range(2):
        copies[half].wait()
        part_ref[half * part : (half + 1) * part, :] = unit_rows(rows[half])


def first_part(embeddings, part):
    features = embeddings.shape[2]
    return pl.pallas_call(
        part_kernel,
        out_shape=jax.ShapeDtypeStruct((2 * part, features), jnp.bfloat16),
        in_specs=[pl.BlockSpec(memory_space=pltpu.HBM)],
        out_specs=pl.BlockSpec(memory_space=pltpu.VMEM),
        scratch_shapes=[
            pltpu.VMEM((2, part, features), jnp.float32),
            pltpu.SemaphoreType.DMA((2,)),
        ],
        compiler_params=pltpu.CompilerParams(vmem_limit_bytes=60 << 20),
        cost_estimate=pl.CostEstimate(
            flops=8 * part * features, bytes_accessed=12 * part * features, transcendentals=2 * part
        ),
        name="first_part",
    )(embeddings)


def key_tables(sizes_ref, counts_ref, groups, part):
    own, place = lax.axis_index("own"), lax.axis_index("pair")
    side = lax.rem(place, 2)
    block_total = counts_ref.shape[0]
    lanes = 2 * part * len(groups)
    bounds = [[jnp.int32(0), jnp.int32(0)] for local in range(2)]
    start = jnp.int32(0)
    for c in range(sizes_ref.shape[0]):
        end = start + sizes_ref[c]
        for local in range(2):
            block = 2 * own + local
            inside = (start <= block) & (block < end)
            bounds[local][0] = jnp.where(inside, start, bounds[local][0])
            bounds[local][1] = jnp.where(inside, end, bounds[local][1])
        start = end
    lane = lax.broadcasted_iota(jnp.int32, (1, lanes), 1)
    piece = lane // part
    sub = lane % part
    row = lax.shift_right_logical(place, 1) * part + sub
    count = jnp.zeros((1, lanes), jnp.int32)
    blocks = jnp.full((1, lanes), -1, jnp.int32)
    for i, offset in enumerate(groups):
        for half in range(2):
            local = side if half else 1 - side
            block = 2 * (own + jnp.where(side == 0, -offset, offset)) + local
            there = (block >= 0) & (block < block_total)
            valid = counts_ref[jnp.clip(block, 0, block_total - 1)]
            here = piece == 2 * i + half
            count = jnp.where(here, jnp.where(there, valid, 0), count)
            blocks = jnp.where(here, block, blocks)
    usable = row < count
    if groups[0] == 0:
        usable = usable & ((lane >= 2 * part) | (sub // (part // 2) == side))
    linked = [
        jnp.where(usable & (blocks >= low) & (blocks < high), 1, 0) for low, high in bounds
    ]
    return blocks * (4 * part) + row, linked


def attend(queries, keys, kept):
    scores = SHARPNESS * lax.dot_general(
        queries, keys, (((1,), (1,)), ((), ())), preferred_element_type=jnp.float32
    )
    scores = jnp.where(kept, scores, NEGATIVE)
    top = jnp.max(scores, axis=1, keepdims=True)
    weight = jnp.where(kept, jnp.exp(scores - top), 0.0)
    mass = jnp.sum(weight, axis=1, keepdims=True)
    total = jnp.dot(weight.astype(jnp.bfloat16), keys, preferred_element_type=jnp.float32)
    return top, mass, total


def near_kernel(sizes_ref, counts_ref, x_ref, *refs):
    *key_refs, q_ref, total_ref, state_ref, far_ref, keys = refs
    step = key_refs[0].shape[0]
    block_rows = x_ref.shape[1]
    rows = q_ref.shape[0]
    for local in range(2):
        q_ref[local * block_rows : (local + 1) * block_rows, :] = unit_rows(x_ref[local])
    for i, ref in enumerate(key_refs):
        keys[i * step : (i + 1) * step, :] = ref[...]
    key_row, linked = key_tables(sizes_ref, counts_ref, list(range(len(key_refs))), step // 2)
    far = key_tables(
        sizes_ref, counts_ref, list(range(len(key_refs), REACH + 1)), step // 2
    )[1]
    for local in range(2):
        far_ref[local : local + 1, :] = far[local]
    query = lax.broadcasted_iota(jnp.int32, (rows, 1), 0)
    kept = jnp.where(query < block_rows, linked[0], linked[1]) != 0
    kept = kept & (key_row != lax.axis_index("own") * rows + query)
    top, mass, total = attend(q_ref[...], keys[...], kept)
    total_ref[...] = total
    lane = lax.broadcasted_iota(jnp.int32, (rows, LANES), 1)
    state_ref[...] = jnp.where(lane == 0, top, mass)


def near_states(cluster_sizes, row_counts, embeddings, near_keys):
    _, block_rows, features = embeddings.shape
    rows = 2 * block_rows
    step = near_keys[0].shape[0]
    key_rows = step * len(near_keys)
    far_rows = step * (REACH + 1 - len(near_keys))
    smem, vmem = (pl.BlockSpec(memory_space=m) for m in (pltpu.SMEM, pltpu.VMEM))
    return pl.pallas_call(
        near_kernel,
        out_shape=(
            jax.ShapeDtypeStruct((rows, features), jnp.bfloat16),
            jax.ShapeDtypeStruct((rows, features), jnp.float32),
            jax.ShapeDtypeStruct((rows, LANES), jnp.float32),
            jax.ShapeDtypeStruct((2, far_rows), jnp.int32),
        ),
        in_specs=[smem, smem] + [vmem] * (1 + len(near_keys)),
        out_specs=(vmem,) * 4,
        scratch_shapes=[pltpu.VMEM((key_rows, features), jnp.bfloat16)],
        compiler_params=pltpu.CompilerParams(vmem_limit_bytes=24 << 20),
        cost_estimate=pl.CostEstimate(
            flops=4 * rows * key_rows * features,
            bytes_accessed=10 * rows * features,
            transcendentals=rows * key_rows,
        ),
        name="near_states",
    )(cluster_sizes, row_counts, embeddings, *near_keys)


def far_kernel(q_ref, total_ref, state_ref, far_ref, *refs):
    *key_refs, out_ref, keys = refs
    step = key_refs[0].shape[0]
    for i, ref in enumerate(key_refs):
        keys[i * step : (i + 1) * step, :] = ref[...]
    rows, features = q_ref.shape
    block_rows = rows // 2
    pair_count = out_ref.shape[0]
    slice_rows = block_rows // pair_count
    query = lax.broadcasted_iota(jnp.int32, (rows, 1), 0)
    kept = jnp.where(query < block_rows, far_ref[0:1, :], far_ref[1:2, :]) != 0
    far_top, far_mass, far_total = attend(q_ref[...], keys[...], kept)
    near_top, near_mass = state_ref[:, 0:1], state_ref[:, 1:2]
    top = jnp.maximum(near_top, far_top)
    near_scale, far_scale = jnp.exp(near_top - top), jnp.exp(far_top - top)
    mass = near_scale * near_mass + far_scale * far_mass
    some = mass > 0.0
    safe = jnp.where(some, mass, 1.0)
    near_scale, far_scale = near_scale / safe, far_scale / safe
    log_mass = jnp.where(some, top + jnp.log(safe), NEGATIVE)
    high = log_mass.astype(jnp.bfloat16).astype(jnp.float32)
    middle = (log_mass - high).astype(jnp.bfloat16).astype(jnp.float32)
    low = log_mass - high - middle
    lane = lax.broadcasted_iota(jnp.int32, (rows, LANES), 1)
    pieces = jnp.where(lane == 0, high, jnp.where(lane == 1, middle, low)).astype(jnp.bfloat16)
    mean = (near_scale * total_ref[...] + far_scale * far_total).astype(jnp.bfloat16)
    for local in range(2):
        for place in range(pair_count):
            first = local * block_rows + place * slice_rows
            here = slice(first, first + slice_rows)
            there = slice(local * slice_rows, (local + 1) * slice_rows)
            out_ref[place, there, 0:features] = mean[here, :]
            out_ref[place, there, features : features + LANES] = pieces[here, :]


def all_states(near, far_keys, pair_count):
    rows, features = near[0].shape
    step = far_keys[0].shape[0]
    key_rows = step * len(far_keys)
    vmem = pl.BlockSpec(memory_space=pltpu.VMEM)
    return pl.pallas_call(
        far_kernel,
        out_shape=jax.ShapeDtypeStruct(
            (pair_count, rows // pair_count, features + LANES), jnp.bfloat16
        ),
        in_specs=[vmem] * (len(near) + len(far_keys)),
        out_specs=vmem,
        scratch_shapes=[pltpu.VMEM((key_rows, features), jnp.bfloat16)],
        compiler_params=pltpu.CompilerParams(vmem_limit_bytes=24 << 20),
        cost_estimate=pl.CostEstimate(
            flops=4 * rows * key_rows * features,
            bytes_accessed=8 * rows * features,
            transcendentals=rows * key_rows,
        ),
        name="all_states",
    )(*near, *far_keys)


def merge_kernel(counts_ref, in_ref, near_ref, log_ref):
    pair_count, rows, wide = in_ref.shape
    features = wide - LANES
    slice_rows = rows // 2
    logs = []
    for i in range(pair_count):
        pieces = in_ref[i, :, features:wide].astype(jnp.float32)
        logs.append(pieces[:, 0:1] + pieces[:, 1:2] + pieces[:, 2:3])
    top = logs[0]
    for one in logs[1:]:
        top = jnp.maximum(top, one)
    scales = [jnp.exp(one - top) for one in logs]
    mass = scales[0]
    for one in scales[1:]:
        mass = mass + one
    share = 1.0 / mass
    near = (scales[0] * share) * in_ref[0, :, 0:features].astype(jnp.float32)
    for i in range(1, pair_count):
        near = near + (scales[i] * share) * in_ref[i, :, 0:features].astype(jnp.float32)
    log_mass = top + jnp.log(mass)
    first = lax.axis_index("pair") * slice_rows
    row = first + lax.broadcasted_iota(jnp.int32, (slice_rows, 1), 0)
    same = lax.broadcasted_iota(jnp.int32, (slice_rows, slice_rows), 0) == lax.broadcasted_iota(
        jnp.int32, (slice_rows, slice_rows), 1
    )
    for local in range(2):
        here = slice(local * slice_rows, (local + 1) * slice_rows)
        valid = row < counts_ref[2 * lax.axis_index("own") + local]
        near_ref[local] = jnp.where(valid, near[here, :], 0.0).astype(near_ref.dtype)
        column = jnp.where(valid, log_mass[here, :], 0.0)
        log_ref[local : local + 1, :] = jnp.sum(
            jnp.where(same, column, 0.0), axis=0, keepdims=True
        )


def merged(counts, arrived):
    pair_count, rows, wide = arrived.shape
    features = wide - LANES
    vmem = pl.BlockSpec(memory_space=pltpu.VMEM)
    return pl.pallas_call(
        merge_kernel,
        out_shape=(
            jax.ShapeDtypeStruct((2, rows // 2, features), jnp.bfloat16),
            jax.ShapeDtypeStruct((2, rows // 2), jnp.float32),
        ),
        in_specs=[pl.BlockSpec(memory_space=pltpu.SMEM), vmem],
        out_specs=(vmem, vmem),
        compiler_params=pltpu.CompilerParams(vmem_limit_bytes=16 << 20),
        cost_estimate=pl.CostEstimate(
            flops=4 * pair_count * rows * features,
            bytes_accessed=2 * (pair_count + 1) * rows * wide,
            transcendentals=pair_count * rows,
        ),
        name="merged",
    )(counts, arrived)


def body(embeddings, cluster_sizes, row_counts):
    block_rows = embeddings.shape[1]
    own_count, pair_count = lax.axis_size("own"), lax.axis_size("pair")
    part = block_rows // (pair_count // 2)

    own_part = first_part(embeddings, part)
    embeddings, own_part = lax.optimization_barrier((embeddings, own_part))
    shards = {by: handed_on(own_part, by, own_count, pair_count) for by in (3, 2, 1)}
    for by in (3, 2, 1):
        shards[3 + by] = handed_on(shards[3], by, own_count, pair_count)
    near = near_states(
        cluster_sizes, row_counts, embeddings, [own_part] + [shards[by] for by in (1, 2, 3)]
    )
    states = all_states(near, [shards[by] for by in (4, 5, 6)], pair_count)
    arrived = lax.all_to_all(states, "pair", split_axis=0, concat_axis=0, tiled=True)
    return merged(row_counts, arrived)


def solution(mesh):
    placed = (P("own", None, None), P(), P())
    return jax.shard_map(
        body,
        mesh=mesh,
        in_specs=placed,
        out_specs=(P("own", "pair", None), P("own", "pair")),
        check_vma=False,
    )
```

```python
import jax
import jax.numpy as jnp
from jax import lax
from jax.experimental import pallas as pl
from jax.experimental.pallas import tpu as pltpu
from jax.sharding import PartitionSpec as P

SHARPNESS = 128.0
NEGATIVE = -1e30
REACH = 6
LANES = 128
STATS = 8
AXES = ("own", "pair")


def handed_on(shard, by, own_count, pair_count):
    pairs = []
    for owner in range(own_count):
        for place in range(pair_count):
            target = owner + (by if place % 2 == 0 else -by)
            if 0 <= target < own_count:
                pairs.append((owner * pair_count + place, target * pair_count + place))
    return lax.ppermute(shard, AXES, pairs)


def unit_rows(values):
    squares = jnp.sum(values * values, axis=-1, keepdims=True)
    return (values * lax.rsqrt(squares + 1e-06)).astype(jnp.bfloat16)


def key_tables(sizes_ref, counts_ref, groups, part):
    own, place = lax.axis_index("own"), lax.axis_index("pair")
    side = lax.rem(place, 2)
    block_total = counts_ref.shape[0]
    lanes = 2 * part * len(groups)
    bounds = [[jnp.int32(0), jnp.int32(0)] for local in range(2)]
    start = jnp.int32(0)
    for c in range(sizes_ref.shape[0]):
        end = start + sizes_ref[c]
        for local in range(2):
            block = 2 * own + local
            inside = (start <= block) & (block < end)
            bounds[local][0] = jnp.where(inside, start, bounds[local][0])
            bounds[local][1] = jnp.where(inside, end, bounds[local][1])
        start = end
    lane = lax.broadcasted_iota(jnp.int32, (1, lanes), 1)
    piece = lane // part
    sub = lane % part
    row = lax.shift_right_logical(place, 1) * part + sub
    count = jnp.zeros((1, lanes), jnp.int32)
    blocks = jnp.full((1, lanes), -1, jnp.int32)
    for i, offset in enumerate(groups):
        for half in range(2):
            block = 2 * (own + jnp.where(side == 0, -offset, offset)) + half
            there = (block >= 0) & (block < block_total)
            valid = counts_ref[jnp.clip(block, 0, block_total - 1)]
            here = piece == 2 * i + half
            count = jnp.where(here, jnp.where(there, valid, 0), count)
            blocks = jnp.where(here, block, blocks)
    usable = row < count
    if groups[0] == 0:
        usable = usable & ((lane >= 2 * part) | (sub // (part // 2) == side))
    linked = [
        jnp.where(usable & (blocks >= low) & (blocks < high), 1, 0) for low, high in bounds
    ]
    return blocks * (4 * part) + row, linked


def attend(queries, keys, kept):
    scores = SHARPNESS * lax.dot_general(
        queries, keys, (((1,), (1,)), ((), ())), preferred_element_type=jnp.float32
    )
    scores = jnp.where(kept, scores, NEGATIVE)
    top = jnp.max(scores, axis=1, keepdims=True)
    weight = jnp.where(kept, jnp.exp(scores - top), 0.0)
    mass = jnp.sum(weight, axis=1, keepdims=True)
    total = jnp.dot(weight.astype(jnp.bfloat16), keys, preferred_element_type=jnp.float32)
    return top, mass, total


def near_kernel(sizes_ref, counts_ref, x_ref, *refs):
    *key_refs, q_ref, total_ref, state_ref, far_ref, keys = refs
    step = key_refs[0].shape[0]
    block_rows = x_ref.shape[1]
    rows = q_ref.shape[0]
    for local in range(2):
        q_ref[local * block_rows : (local + 1) * block_rows, :] = unit_rows(x_ref[local])
    for i, ref in enumerate(key_refs):
        keys[i * step : (i + 1) * step, :] = ref[...]
    key_row, linked = key_tables(sizes_ref, counts_ref, list(range(len(key_refs))), step // 2)
    far = key_tables(
        sizes_ref, counts_ref, list(range(len(key_refs), REACH + 1)), step // 2
    )[1]
    for local in range(2):
        far_ref[local : local + 1, :] = far[local]
    query = lax.broadcasted_iota(jnp.int32, (rows, 1), 0)
    kept = jnp.where(query < block_rows, linked[0], linked[1]) != 0
    kept = kept & (key_row != lax.axis_index("own") * rows + query)
    top, mass, total = attend(q_ref[...], keys[...], kept)
    total_ref[...] = total
    lane = lax.broadcasted_iota(jnp.int32, (rows, LANES), 1)
    state_ref[...] = jnp.where(lane == 0, top, mass)


def near_states(cluster_sizes, row_counts, embeddings, near_keys):
    _, block_rows, features = embeddings.shape
    rows = 2 * block_rows
    step = near_keys[0].shape[0]
    key_rows = step * len(near_keys)
    far_rows = step * (REACH + 1 - len(near_keys))
    smem, vmem = (pl.BlockSpec(memory_space=m) for m in (pltpu.SMEM, pltpu.VMEM))
    return pl.pallas_call(
        near_kernel,
        out_shape=(
            jax.ShapeDtypeStruct((rows, features), jnp.bfloat16),
            jax.ShapeDtypeStruct((rows, features), jnp.float32),
            jax.ShapeDtypeStruct((rows, LANES), jnp.float32),
            jax.ShapeDtypeStruct((2, far_rows), jnp.int32),
        ),
        in_specs=[smem, smem] + [vmem] * (1 + len(near_keys)),
        out_specs=(vmem,) * 4,
        scratch_shapes=[pltpu.VMEM((key_rows, features), jnp.bfloat16)],
        compiler_params=pltpu.CompilerParams(vmem_limit_bytes=24 << 20),
        cost_estimate=pl.CostEstimate(
            flops=4 * rows * key_rows * features,
            bytes_accessed=10 * rows * features,
            transcendentals=rows * key_rows,
        ),
        name="near_states",
    )(cluster_sizes, row_counts, embeddings, *near_keys)


def far_kernel(q_ref, total_ref, state_ref, far_ref, *refs):
    *key_refs, out_ref, keys = refs
    step = key_refs[0].shape[0]
    for i, ref in enumerate(key_refs):
        keys[i * step : (i + 1) * step, :] = ref[...]
    rows, features = q_ref.shape
    block_rows = rows // 2
    pair_count = out_ref.shape[0]
    slice_rows = block_rows // pair_count
    query = lax.broadcasted_iota(jnp.int32, (rows, 1), 0)
    kept = jnp.where(query < block_rows, far_ref[0:1, :], far_ref[1:2, :]) != 0
    far_top, far_mass, far_total = attend(q_ref[...], keys[...], kept)
    near_top, near_mass = state_ref[:, 0:1], state_ref[:, 1:2]
    top = jnp.maximum(near_top, far_top)
    near_scale, far_scale = jnp.exp(near_top - top), jnp.exp(far_top - top)
    mass = near_scale * near_mass + far_scale * far_mass
    some = mass > 0.0
    safe = jnp.where(some, mass, 1.0)
    near_scale, far_scale = near_scale / safe, far_scale / safe
    log_mass = jnp.where(some, top + jnp.log(safe), NEGATIVE)
    mean = (near_scale * total_ref[...] + far_scale * far_total).astype(jnp.bfloat16)
    across = lax.broadcasted_iota(jnp.int32, (block_rows, block_rows), 0)
    across = across == lax.broadcasted_iota(jnp.int32, (block_rows, block_rows), 1)
    line = lax.broadcasted_iota(jnp.int32, (STATS, block_rows), 0)
    pieces = jnp.zeros((STATS, block_rows), jnp.float32)
    for local in range(2):
        column = log_mass[local * block_rows : (local + 1) * block_rows, :]
        logs = jnp.sum(jnp.where(across, column, 0.0), axis=0, keepdims=True)
        high = logs.astype(jnp.bfloat16).astype(jnp.float32)
        middle = (logs - high).astype(jnp.bfloat16).astype(jnp.float32)
        for i, piece in enumerate((high, middle, logs - high - middle)):
            pieces = jnp.where(line == 3 * local + i, piece, pieces)
    pieces = pieces.astype(jnp.bfloat16)
    for place in range(pair_count):
        for local in range(2):
            first = local * block_rows + place * slice_rows
            for i in range(features // LANES):
                there = (2 * i + local) * slice_rows
                out_ref[place, there : there + slice_rows, :] = mean[
                    first : first + slice_rows, i * LANES : (i + 1) * LANES
                ]
        tail = 2 * slice_rows * (features // LANES)
        out_ref[place, tail : tail + STATS, :] = pieces


def all_states(near, far_keys, pair_count):
    rows, features = near[0].shape
    step = far_keys[0].shape[0]
    key_rows = step * len(far_keys)
    vmem = pl.BlockSpec(memory_space=pltpu.VMEM)
    return pl.pallas_call(
        far_kernel,
        out_shape=jax.ShapeDtypeStruct(
            (pair_count, rows // pair_count * (features // LANES) + STATS, LANES), jnp.bfloat16
        ),
        in_specs=[vmem] * (len(near) + len(far_keys)),
        out_specs=vmem,
        scratch_shapes=[pltpu.VMEM((key_rows, features), jnp.bfloat16)],
        compiler_params=pltpu.CompilerParams(vmem_limit_bytes=24 << 20),
        cost_estimate=pl.CostEstimate(
            flops=4 * rows * key_rows * features,
            bytes_accessed=8 * rows * features,
            transcendentals=rows * key_rows,
        ),
        name="all_states",
    )(*near, *far_keys)


def merge_kernel(counts_ref, in_ref, near_ref, log_ref):
    pair_count, lines, _ = in_ref.shape
    slice_rows, features = near_ref.shape[1:]
    tail = lines - STATS
    place = lax.axis_index("pair")
    first = place * slice_rows
    lane = lax.broadcasted_iota(jnp.int32, (slice_rows, LANES), 1)
    picked = lane == first + lax.broadcasted_iota(jnp.int32, (slice_rows, LANES), 0)
    row = first + lax.broadcasted_iota(jnp.int32, (slice_rows, 1), 0)
    square = lax.broadcasted_iota(jnp.int32, (slice_rows, slice_rows), 0)
    square = square == lax.broadcasted_iota(jnp.int32, (slice_rows, slice_rows), 1)
    tiles = [in_ref[i, tail:lines, :].astype(jnp.float32) for i in range(pair_count)]
    for local in range(2):
        at = 3 * local
        logs = [
            tile[at : at + 1, :] + tile[at + 1 : at + 2, :] + tile[at + 2 : at + 3, :]
            for tile in tiles
        ]
        top = logs[0]
        for one in logs[1:]:
            top = jnp.maximum(top, one)
        scales = [jnp.exp(one - top) for one in logs]
        mass = scales[0]
        for one in scales[1:]:
            mass = mass + one
        share = 1.0 / mass
        columns = [
            jnp.sum(jnp.where(picked, scale * share, 0.0), axis=1, keepdims=True)
            for scale in scales
        ]
        valid = row < counts_ref[2 * lax.axis_index("own") + local]
        for i in range(features // LANES):
            there = (2 * i + local) * slice_rows
            here = slice(there, there + slice_rows)
            near = columns[0] * in_ref[0, here, :].astype(jnp.float32)
            for j in range(1, pair_count):
                near = near + columns[j] * in_ref[j, here, :].astype(jnp.float32)
            near_ref[local, :, i * LANES : (i + 1) * LANES] = jnp.where(valid, near, 0.0).astype(
                near_ref.dtype
            )
        column = jnp.sum(jnp.where(picked, top + jnp.log(mass), 0.0), axis=1, keepdims=True)
        column = jnp.where(valid, column, 0.0)
        log_ref[local : local + 1, :] = jnp.sum(
            jnp.where(square, column, 0.0), axis=0, keepdims=True
        )


def merged(counts, arrived, rows, features):
    pair_count = arrived.shape[0]
    vmem = pl.BlockSpec(memory_space=pltpu.VMEM)
    return pl.pallas_call(
        merge_kernel,
        out_shape=(
            jax.ShapeDtypeStruct((2, rows, features), jnp.bfloat16),
            jax.ShapeDtypeStruct((2, rows), jnp.float32),
        ),
        in_specs=[pl.BlockSpec(memory_space=pltpu.SMEM), vmem],
        out_specs=(vmem, vmem),
        compiler_params=pltpu.CompilerParams(vmem_limit_bytes=16 << 20),
        cost_estimate=pl.CostEstimate(
            flops=8 * pair_count * rows * features,
            bytes_accessed=4 * (pair_count + 1) * rows * features,
            transcendentals=2 * pair_count * rows,
        ),
        name="merged",
    )(counts, arrived)


def body(embeddings, cluster_sizes, row_counts):
    block_rows = embeddings.shape[1]
    own_count, pair_count = lax.axis_size("own"), lax.axis_size("pair")
    part = block_rows // (pair_count // 2)

    start = (lax.axis_index("pair") // 2) * part
    own_part = unit_rows(lax.dynamic_slice_in_dim(embeddings, start, part, 1))
    own_part = own_part.reshape(2 * part, embeddings.shape[2])
    embeddings, own_part = lax.optimization_barrier((embeddings, own_part))
    shards = {by: handed_on(own_part, by, own_count, pair_count) for by in (3, 2, 1)}
    for by in (3, 2, 1):
        shards[3 + by] = handed_on(shards[3], by, own_count, pair_count)
    near = near_states(
        cluster_sizes, row_counts, embeddings, [own_part] + [shards[by] for by in (1, 2, 3)]
    )
    states = all_states(near, [shards[by] for by in (4, 5, 6)], pair_count)
    arrived = lax.all_to_all(states, "pair", split_axis=0, concat_axis=0, tiled=True)
    return merged(row_counts, arrived, block_rows // pair_count, embeddings.shape[2])


def solution(mesh):
    placed = (P("own", None, None), P(), P())
    return jax.shard_map(
        body,
        mesh=mesh,
        in_specs=placed,
        out_specs=(P("own", "pair", None), P("own", "pair")),
        check_vma=False,
    )
```

```python
import jax
import jax.numpy as jnp
from jax import lax
from jax.experimental import pallas as pl
from jax.experimental.pallas import tpu as pltpu
from jax.sharding import PartitionSpec as P

SHARPNESS = 128.0
NEGATIVE = -1e30
REACH = 6
LANES = 128
STATS = 8
AXES = ("own", "pair")


def handed_on(shard, by, own_count, pair_count):
    pairs = []
    for owner in range(own_count):
        for place in range(pair_count):
            target = owner + (by if place % 2 == 0 else -by)
            if 0 <= target < own_count:
                pairs.append((owner * pair_count + place, target * pair_count + place))
    return lax.ppermute(shard, AXES, pairs)


def unit_rows(values):
    squares = jnp.sum(values * values, axis=-1, keepdims=True)
    return (values * lax.rsqrt(squares + 1e-06)).astype(jnp.bfloat16)


def part_kernel(x_ref, part_ref, rows, sems):
    part = rows.shape[1]
    place = lax.axis_index("pair")
    start = pl.multiple_of(lax.shift_right_logical(place, 1) * part, part)
    copies = []
    for half in range(2):
        copies.append(
            pltpu.make_async_copy(
                x_ref.at[half, pl.ds(start, part), :], rows.at[half], sems.at[half]
            )
        )
        copies[half].start()
    for half in range(2):
        copies[half].wait()
        part_ref[half * part : (half + 1) * part, :] = unit_rows(rows[half])


def first_part(embeddings, part):
    features = embeddings.shape[2]
    return pl.pallas_call(
        part_kernel,
        out_shape=jax.ShapeDtypeStruct((2 * part, features), jnp.bfloat16),
        in_specs=[pl.BlockSpec(memory_space=pltpu.HBM)],
        out_specs=pl.BlockSpec(memory_space=pltpu.VMEM),
        scratch_shapes=[
            pltpu.VMEM((2, part, features), jnp.float32),
            pltpu.SemaphoreType.DMA((2,)),
        ],
        compiler_params=pltpu.CompilerParams(vmem_limit_bytes=4 << 20),
        cost_estimate=pl.CostEstimate(
            flops=8 * part * features, bytes_accessed=12 * part * features, transcendentals=2 * part
        ),
        name="first_part",
    )(pltpu.with_memory_space_constraint(embeddings, pltpu.HBM))


def key_tables(sizes_ref, counts_ref, groups, part):
    own, place = lax.axis_index("own"), lax.axis_index("pair")
    side = lax.rem(place, 2)
    block_total = counts_ref.shape[0]
    lanes = 2 * part * len(groups)
    bounds = [[jnp.int32(0), jnp.int32(0)] for local in range(2)]
    start = jnp.int32(0)
    for c in range(sizes_ref.shape[0]):
        end = start + sizes_ref[c]
        for local in range(2):
            block = 2 * own + local
            inside = (start <= block) & (block < end)
            bounds[local][0] = jnp.where(inside, start, bounds[local][0])
            bounds[local][1] = jnp.where(inside, end, bounds[local][1])
        start = end
    lane = lax.broadcasted_iota(jnp.int32, (1, lanes), 1)
    piece = lane // part
    sub = lane % part
    row = lax.shift_right_logical(place, 1) * part + sub
    count = jnp.zeros((1, lanes), jnp.int32)
    blocks = jnp.full((1, lanes), -1, jnp.int32)
    for i, offset in enumerate(groups):
        for half in range(2):
            block = 2 * (own + jnp.where(side == 0, -offset, offset)) + half
            there = (block >= 0) & (block < block_total)
            valid = counts_ref[jnp.clip(block, 0, block_total - 1)]
            here = piece == 2 * i + half
            count = jnp.where(here, jnp.where(there, valid, 0), count)
            blocks = jnp.where(here, block, blocks)
    usable = row < count
    if groups[0] == 0:
        usable = usable & ((lane >= 2 * part) | (sub // (part // 2) == side))
    linked = [
        jnp.where(usable & (blocks >= low) & (blocks < high), 1, 0) for low, high in bounds
    ]
    return blocks * (4 * part) + row, linked


def attend(queries, keys, kept):
    scores = SHARPNESS * lax.dot_general(
        queries, keys, (((1,), (1,)), ((), ())), preferred_element_type=jnp.float32
    )
    scores = jnp.where(kept, scores, NEGATIVE)
    top = jnp.max(scores, axis=1, keepdims=True)
    weight = jnp.where(kept, jnp.exp(scores - top), 0.0)
    mass = jnp.sum(weight, axis=1, keepdims=True)
    total = jnp.dot(weight.astype(jnp.bfloat16), keys, preferred_element_type=jnp.float32)
    return top, mass, total


def near_kernel(sizes_ref, counts_ref, x_ref, *refs):
    *key_refs, q_ref, total_ref, state_ref, far_ref, keys = refs
    step = key_refs[0].shape[0]
    block_rows = x_ref.shape[1]
    rows = q_ref.shape[0]
    for local in range(2):
        q_ref[local * block_rows : (local + 1) * block_rows, :] = unit_rows(x_ref[local])
    for i, ref in enumerate(key_refs):
        keys[i * step : (i + 1) * step, :] = ref[...]
    key_row, linked = key_tables(sizes_ref, counts_ref, list(range(len(key_refs))), step // 2)
    far = key_tables(
        sizes_ref, counts_ref, list(range(len(key_refs), REACH + 1)), step // 2
    )[1]
    for local in range(2):
        far_ref[local : local + 1, :] = far[local]
    query = lax.broadcasted_iota(jnp.int32, (rows, 1), 0)
    kept = jnp.where(query < block_rows, linked[0], linked[1]) != 0
    kept = kept & (key_row != lax.axis_index("own") * rows + query)
    top, mass, total = attend(q_ref[...], keys[...], kept)
    total_ref[...] = total
    lane = lax.broadcasted_iota(jnp.int32, (rows, LANES), 1)
    state_ref[...] = jnp.where(lane == 0, top, mass)


def near_states(cluster_sizes, row_counts, embeddings, near_keys):
    _, block_rows, features = embeddings.shape
    rows = 2 * block_rows
    step = near_keys[0].shape[0]
    key_rows = step * len(near_keys)
    far_rows = step * (REACH + 1 - len(near_keys))
    smem, vmem = (pl.BlockSpec(memory_space=m) for m in (pltpu.SMEM, pltpu.VMEM))
    return pl.pallas_call(
        near_kernel,
        out_shape=(
            jax.ShapeDtypeStruct((rows, features), jnp.bfloat16),
            jax.ShapeDtypeStruct((rows, features), jnp.float32),
            jax.ShapeDtypeStruct((rows, LANES), jnp.float32),
            jax.ShapeDtypeStruct((2, far_rows), jnp.int32),
        ),
        in_specs=[smem, smem] + [vmem] * (1 + len(near_keys)),
        out_specs=(vmem,) * 4,
        scratch_shapes=[pltpu.VMEM((key_rows, features), jnp.bfloat16)],
        compiler_params=pltpu.CompilerParams(vmem_limit_bytes=24 << 20),
        cost_estimate=pl.CostEstimate(
            flops=4 * rows * key_rows * features,
            bytes_accessed=10 * rows * features,
            transcendentals=rows * key_rows,
        ),
        name="near_states",
    )(cluster_sizes, row_counts, embeddings, *near_keys)


def far_kernel(q_ref, total_ref, state_ref, far_ref, *refs):
    *key_refs, out_ref, keys = refs
    step = key_refs[0].shape[0]
    for i, ref in enumerate(key_refs):
        keys[i * step : (i + 1) * step, :] = ref[...]
    rows, features = q_ref.shape
    block_rows = rows // 2
    pair_count = out_ref.shape[0]
    slice_rows = block_rows // pair_count
    query = lax.broadcasted_iota(jnp.int32, (rows, 1), 0)
    kept = jnp.where(query < block_rows, far_ref[0:1, :], far_ref[1:2, :]) != 0
    far_top, far_mass, far_total = attend(q_ref[...], keys[...], kept)
    near_top, near_mass = state_ref[:, 0:1], state_ref[:, 1:2]
    top = jnp.maximum(near_top, far_top)
    near_scale, far_scale = jnp.exp(near_top - top), jnp.exp(far_top - top)
    mass = near_scale * near_mass + far_scale * far_mass
    some = mass > 0.0
    safe = jnp.where(some, mass, 1.0)
    near_scale, far_scale = near_scale / safe, far_scale / safe
    log_mass = jnp.where(some, top + jnp.log(safe), NEGATIVE)
    mean = (near_scale * total_ref[...] + far_scale * far_total).astype(jnp.bfloat16)
    across = lax.broadcasted_iota(jnp.int32, (block_rows, block_rows), 0)
    across = across == lax.broadcasted_iota(jnp.int32, (block_rows, block_rows), 1)
    line = lax.broadcasted_iota(jnp.int32, (STATS, block_rows), 0)
    pieces = jnp.zeros((STATS, block_rows), jnp.float32)
    for local in range(2):
        column = log_mass[local * block_rows : (local + 1) * block_rows, :]
        logs = jnp.sum(jnp.where(across, column, 0.0), axis=0, keepdims=True)
        high = logs.astype(jnp.bfloat16).astype(jnp.float32)
        middle = (logs - high).astype(jnp.bfloat16).astype(jnp.float32)
        for i, piece in enumerate((high, middle, logs - high - middle)):
            pieces = jnp.where(line == 3 * local + i, piece, pieces)
    pieces = pieces.astype(jnp.bfloat16)
    for place in range(pair_count):
        for local in range(2):
            first = local * block_rows + place * slice_rows
            for i in range(features // LANES):
                there = (2 * i + local) * slice_rows
                out_ref[place, there : there + slice_rows, :] = mean[
                    first : first + slice_rows, i * LANES : (i + 1) * LANES
                ]
        tail = 2 * slice_rows * (features // LANES)
        out_ref[place, tail : tail + STATS, :] = pieces


def all_states(near, far_keys, pair_count):
    rows, features = near[0].shape
    step = far_keys[0].shape[0]
    key_rows = step * len(far_keys)
    vmem = pl.BlockSpec(memory_space=pltpu.VMEM)
    return pl.pallas_call(
        far_kernel,
        out_shape=jax.ShapeDtypeStruct(
            (pair_count, rows // pair_count * (features // LANES) + STATS, LANES), jnp.bfloat16
        ),
        in_specs=[vmem] * (len(near) + len(far_keys)),
        out_specs=vmem,
        scratch_shapes=[pltpu.VMEM((key_rows, features), jnp.bfloat16)],
        compiler_params=pltpu.CompilerParams(vmem_limit_bytes=24 << 20),
        cost_estimate=pl.CostEstimate(
            flops=4 * rows * key_rows * features,
            bytes_accessed=8 * rows * features,
            transcendentals=rows * key_rows,
        ),
        name="all_states",
    )(*near, *far_keys)


def merge_kernel(counts_ref, in_ref, near_out, log_ref, near_ref, sems):
    pair_count, lines, _ = in_ref.shape
    slice_rows, features = near_ref.shape[1:]
    tail = lines - STATS
    place = lax.axis_index("pair")
    first = place * slice_rows
    lane = lax.broadcasted_iota(jnp.int32, (slice_rows, LANES), 1)
    picked = lane == first + lax.broadcasted_iota(jnp.int32, (slice_rows, LANES), 0)
    row = first + lax.broadcasted_iota(jnp.int32, (slice_rows, 1), 0)
    square = lax.broadcasted_iota(jnp.int32, (slice_rows, slice_rows), 0)
    square = square == lax.broadcasted_iota(jnp.int32, (slice_rows, slice_rows), 1)
    tiles = [in_ref[i, tail:lines, :].astype(jnp.float32) for i in range(pair_count)]
    writes = []
    for local in range(2):
        at = 3 * local
        logs = [
            tile[at : at + 1, :] + tile[at + 1 : at + 2, :] + tile[at + 2 : at + 3, :]
            for tile in tiles
        ]
        top = logs[0]
        for one in logs[1:]:
            top = jnp.maximum(top, one)
        scales = [jnp.exp(one - top) for one in logs]
        mass = scales[0]
        for one in scales[1:]:
            mass = mass + one
        share = 1.0 / mass
        columns = [
            jnp.sum(jnp.where(picked, scale * share, 0.0), axis=1, keepdims=True)
            for scale in scales
        ]
        valid = row < counts_ref[2 * lax.axis_index("own") + local]
        for i in range(features // LANES):
            there = (2 * i + local) * slice_rows
            here = slice(there, there + slice_rows)
            near = columns[0] * in_ref[0, here, :].astype(jnp.float32)
            for j in range(1, pair_count):
                near = near + columns[j] * in_ref[j, here, :].astype(jnp.float32)
            near_ref[local, :, i * LANES : (i + 1) * LANES] = jnp.where(valid, near, 0.0).astype(
                near_ref.dtype
            )
        writes.append(
            pltpu.make_async_copy(near_ref.at[local], near_out.at[local], sems.at[local])
        )
        writes[local].start()
        column = jnp.sum(jnp.where(picked, top + jnp.log(mass), 0.0), axis=1, keepdims=True)
        column = jnp.where(valid, column, 0.0)
        log_ref[local : local + 1, :] = jnp.sum(
            jnp.where(square, column, 0.0), axis=0, keepdims=True
        )
    for write in writes:
        write.wait()


def merged(counts, arrived, rows, features):
    pair_count = arrived.shape[0]
    vmem = pl.BlockSpec(memory_space=pltpu.VMEM)
    return pl.pallas_call(
        merge_kernel,
        out_shape=(
            jax.ShapeDtypeStruct((2, rows, features), jnp.bfloat16),
            jax.ShapeDtypeStruct((2, rows), jnp.float32),
        ),
        in_specs=[pl.BlockSpec(memory_space=pltpu.SMEM), vmem],
        out_specs=(pl.BlockSpec(memory_space=pltpu.HBM), vmem),
        scratch_shapes=[
            pltpu.VMEM((2, rows, features), jnp.bfloat16),
            pltpu.SemaphoreType.DMA((2,)),
        ],
        compiler_params=pltpu.CompilerParams(vmem_limit_bytes=16 << 20),
        cost_estimate=pl.CostEstimate(
            flops=8 * pair_count * rows * features,
            bytes_accessed=4 * (pair_count + 1) * rows * features,
            transcendentals=2 * pair_count * rows,
        ),
        name="merged",
    )(counts, arrived)


def body(embeddings, cluster_sizes, row_counts):
    block_rows = embeddings.shape[1]
    own_count, pair_count = lax.axis_size("own"), lax.axis_size("pair")
    part = block_rows // (pair_count // 2)

    own_part = first_part(embeddings, part)
    embeddings, own_part = lax.optimization_barrier((embeddings, own_part))
    shards = {by: handed_on(own_part, by, own_count, pair_count) for by in (3, 2, 1)}
    for by in (3, 2, 1):
        shards[3 + by] = handed_on(shards[3], by, own_count, pair_count)
    near = near_states(
        cluster_sizes, row_counts, embeddings, [own_part] + [shards[by] for by in (1, 2, 3)]
    )
    states = all_states(near, [shards[by] for by in (4, 5, 6)], pair_count)
    arrived = lax.all_to_all(states, "pair", split_axis=0, concat_axis=0, tiled=True)
    return merged(row_counts, arrived, block_rows // pair_count, embeddings.shape[2])


def solution(mesh):
    placed = (P("own", None, None), P(), P())
    return jax.shard_map(
        body,
        mesh=mesh,
        in_specs=placed,
        out_specs=(P("own", "pair", None), P("own", "pair")),
        check_vma=False,
    )
```

```python
import jax
import jax.numpy as jnp
from jax import lax
from jax.experimental import pallas as pl
from jax.experimental.pallas import tpu as pltpu
from jax.sharding import PartitionSpec as P

SHARPNESS = 128.0
NEGATIVE = -1e30
NEAR = ((0, 0), (0, 1), (1, 0), (1, 1), (3, 0), (3, 1))
FAR = ((5, 0), (5, 1), (2, 0), (2, 1), (4, 0), (4, 1), (6, 0))
LANES = 128
STATS = 8
AXES = ("own", "pair")


def handed_on(shard, by, own_count, pair_count):
    pairs = []
    for owner in range(own_count):
        for place in range(pair_count):
            target = owner + (by if place % 2 == 0 else -by)
            if 0 <= target < own_count:
                pairs.append((owner * pair_count + place, target * pair_count + place))
    return lax.ppermute(shard, AXES, pairs)


def unit_rows(values):
    squares = jnp.sum(values * values, axis=-1, keepdims=True)
    return (values * lax.rsqrt(squares + 1e-06)).astype(jnp.bfloat16)


def part_kernel(x_ref, part_ref, rows, sems):
    part = rows.shape[1]
    place = lax.axis_index("pair")
    side = lax.rem(place, 2)
    start = pl.multiple_of(lax.shift_right_logical(place, 1) * part, part)
    copies = []
    for half in range(2):
        copies.append(
            pltpu.make_async_copy(
                x_ref.at[side if half else 1 - side, pl.ds(start, part), :], rows.at[half], sems.at[half]
            )
        )
        copies[half].start()
    for half in range(2):
        copies[half].wait()
        part_ref[half * part : (half + 1) * part, :] = unit_rows(rows[half])


def first_part(embeddings, part):
    features = embeddings.shape[2]
    return pl.pallas_call(
        part_kernel,
        out_shape=jax.ShapeDtypeStruct((2 * part, features), jnp.bfloat16),
        in_specs=[pl.BlockSpec(memory_space=pltpu.HBM)],
        out_specs=pl.BlockSpec(memory_space=pltpu.VMEM),
        scratch_shapes=[
            pltpu.VMEM((2, part, features), jnp.float32),
            pltpu.SemaphoreType.DMA((2,)),
        ],
        compiler_params=pltpu.CompilerParams(vmem_limit_bytes=4 << 20),
        cost_estimate=pl.CostEstimate(
            flops=8 * part * features, bytes_accessed=12 * part * features, transcendentals=2 * part
        ),
        name="first_part",
    )(pltpu.with_memory_space_constraint(embeddings, pltpu.HBM))


def key_tables(sizes_ref, counts_ref, pieces, part):
    own, place = lax.axis_index("own"), lax.axis_index("pair")
    side = lax.rem(place, 2)
    block_total = counts_ref.shape[0]
    lanes = part * len(pieces)
    bounds = [[jnp.int32(0), jnp.int32(0)] for local in range(2)]
    start = jnp.int32(0)
    for c in range(sizes_ref.shape[0]):
        end = start + sizes_ref[c]
        for local in range(2):
            block = 2 * own + local
            inside = (start <= block) & (block < end)
            bounds[local][0] = jnp.where(inside, start, bounds[local][0])
            bounds[local][1] = jnp.where(inside, end, bounds[local][1])
        start = end
    lane = lax.broadcasted_iota(jnp.int32, (1, lanes), 1)
    piece = lane // part
    sub = lane % part
    row = lax.shift_right_logical(place, 1) * part + sub
    count = jnp.zeros((1, lanes), jnp.int32)
    blocks = jnp.full((1, lanes), -1, jnp.int32)
    for i, (offset, half) in enumerate(pieces):
        block = 2 * (own + jnp.where(side == 0, -offset, offset)) + (side if half else 1 - side)
        there = (block >= 0) & (block < block_total)
        valid = counts_ref[jnp.clip(block, 0, block_total - 1)]
        here = piece == i
        count = jnp.where(here, jnp.where(there, valid, 0), count)
        blocks = jnp.where(here, block, blocks)
    usable = row < count
    if pieces[0][0] == 0:
        usable = usable & ((lane >= 2 * part) | (sub // (part // 2) == side))
    linked = [
        jnp.where(usable & (blocks >= low) & (blocks < high), 1, 0) for low, high in bounds
    ]
    return blocks * (4 * part) + row, linked


def attend(queries, keys, kept):
    scores = SHARPNESS * lax.dot_general(
        queries, keys, (((1,), (1,)), ((), ())), preferred_element_type=jnp.float32
    )
    scores = jnp.where(kept, scores, NEGATIVE)
    top = jnp.max(scores, axis=1, keepdims=True)
    weight = jnp.where(kept, jnp.exp(scores - top), 0.0)
    mass = jnp.sum(weight, axis=1, keepdims=True)
    total = jnp.dot(weight.astype(jnp.bfloat16), keys, preferred_element_type=jnp.float32)
    return top, mass, total


def gathered(keys, refs):
    start = 0
    for ref in refs:
        keys[start : start + ref.shape[0], :] = ref[...]
        start += ref.shape[0]


def near_kernel(sizes_ref, counts_ref, x_ref, *refs):
    *key_refs, q_ref, total_ref, state_ref, far_ref, keys = refs
    part = key_refs[0].shape[0] // 2
    block_rows = x_ref.shape[1]
    rows = q_ref.shape[0]
    for local in range(2):
        q_ref[local * block_rows : (local + 1) * block_rows, :] = unit_rows(x_ref[local])
    gathered(keys, key_refs)
    key_row, linked = key_tables(sizes_ref, counts_ref, NEAR, part)
    far = key_tables(sizes_ref, counts_ref, FAR, part)[1]
    for local in range(2):
        far_ref[local : local + 1, :] = far[local]
    query = lax.broadcasted_iota(jnp.int32, (rows, 1), 0)
    kept = jnp.where(query < block_rows, linked[0], linked[1]) != 0
    kept = kept & (key_row != lax.axis_index("own") * rows + query)
    top, mass, total = attend(q_ref[...], keys[...], kept)
    total_ref[...] = total
    lane = lax.broadcasted_iota(jnp.int32, (rows, LANES), 1)
    state_ref[...] = jnp.where(lane == 0, top, mass)


def near_states(cluster_sizes, row_counts, embeddings, near_keys):
    _, block_rows, features = embeddings.shape
    rows = 2 * block_rows
    part = near_keys[0].shape[0] // 2
    key_rows = part * len(NEAR)
    far_rows = part * len(FAR)
    smem, vmem = (pl.BlockSpec(memory_space=m) for m in (pltpu.SMEM, pltpu.VMEM))
    return pl.pallas_call(
        near_kernel,
        out_shape=(
            jax.ShapeDtypeStruct((rows, features), jnp.bfloat16),
            jax.ShapeDtypeStruct((rows, features), jnp.float32),
            jax.ShapeDtypeStruct((rows, LANES), jnp.float32),
            jax.ShapeDtypeStruct((2, far_rows), jnp.int32),
        ),
        in_specs=[smem, smem] + [vmem] * (1 + len(near_keys)),
        out_specs=(vmem,) * 4,
        scratch_shapes=[pltpu.VMEM((key_rows, features), jnp.bfloat16)],
        compiler_params=pltpu.CompilerParams(vmem_limit_bytes=24 << 20),
        cost_estimate=pl.CostEstimate(
            flops=4 * rows * key_rows * features,
            bytes_accessed=10 * rows * features,
            transcendentals=rows * key_rows,
        ),
        name="near_states",
    )(cluster_sizes, row_counts, embeddings, *near_keys)


def far_kernel(q_ref, total_ref, state_ref, far_ref, *refs):
    *key_refs, out_ref, keys = refs
    gathered(keys, key_refs)
    rows, features = q_ref.shape
    block_rows = rows // 2
    pair_count = out_ref.shape[0]
    slice_rows = block_rows // pair_count
    query = lax.broadcasted_iota(jnp.int32, (rows, 1), 0)
    kept = jnp.where(query < block_rows, far_ref[0:1, :], far_ref[1:2, :]) != 0
    far_top, far_mass, far_total = attend(q_ref[...], keys[...], kept)
    near_top, near_mass = state_ref[:, 0:1], state_ref[:, 1:2]
    top = jnp.maximum(near_top, far_top)
    near_scale, far_scale = jnp.exp(near_top - top), jnp.exp(far_top - top)
    mass = near_scale * near_mass + far_scale * far_mass
    some = mass > 0.0
    safe = jnp.where(some, mass, 1.0)
    near_scale, far_scale = near_scale / safe, far_scale / safe
    log_mass = jnp.where(some, top + jnp.log(safe), NEGATIVE)
    mean = (near_scale * total_ref[...] + far_scale * far_total).astype(jnp.bfloat16)
    across = lax.broadcasted_iota(jnp.int32, (block_rows, block_rows), 0)
    across = across == lax.broadcasted_iota(jnp.int32, (block_rows, block_rows), 1)
    line = lax.broadcasted_iota(jnp.int32, (STATS, block_rows), 0)
    pieces = jnp.zeros((STATS, block_rows), jnp.float32)
    for local in range(2):
        column = log_mass[local * block_rows : (local + 1) * block_rows, :]
        logs = jnp.sum(jnp.where(across, column, 0.0), axis=0, keepdims=True)
        high = logs.astype(jnp.bfloat16).astype(jnp.float32)
        middle = (logs - high).astype(jnp.bfloat16).astype(jnp.float32)
        for i, piece in enumerate((high, middle, logs - high - middle)):
            pieces = jnp.where(line == 3 * local + i, piece, pieces)
    pieces = pieces.astype(jnp.bfloat16)
    for place in range(pair_count):
        for local in range(2):
            first = local * block_rows + place * slice_rows
            for i in range(features // LANES):
                there = (2 * i + local) * slice_rows
                out_ref[place, there : there + slice_rows, :] = mean[
                    first : first + slice_rows, i * LANES : (i + 1) * LANES
                ]
        tail = 2 * slice_rows * (features // LANES)
        out_ref[place, tail : tail + STATS, :] = pieces


def all_states(near, far_keys, pair_count):
    rows, features = near[0].shape
    key_rows = sum(keys.shape[0] for keys in far_keys)
    vmem = pl.BlockSpec(memory_space=pltpu.VMEM)
    return pl.pallas_call(
        far_kernel,
        out_shape=jax.ShapeDtypeStruct(
            (pair_count, rows // pair_count * (features // LANES) + STATS, LANES), jnp.bfloat16
        ),
        in_specs=[vmem] * (len(near) + len(far_keys)),
        out_specs=vmem,
        scratch_shapes=[pltpu.VMEM((key_rows, features), jnp.bfloat16)],
        compiler_params=pltpu.CompilerParams(vmem_limit_bytes=24 << 20),
        cost_estimate=pl.CostEstimate(
            flops=4 * rows * key_rows * features,
            bytes_accessed=8 * rows * features,
            transcendentals=rows * key_rows,
        ),
        name="all_states",
    )(*near, *far_keys)


def merge_kernel(counts_ref, in_ref, near_ref, log_ref):
    pair_count, lines, _ = in_ref.shape
    slice_rows, features = near_ref.shape[1:]
    tail = lines - STATS
    place = lax.axis_index("pair")
    first = place * slice_rows
    lane = lax.broadcasted_iota(jnp.int32, (slice_rows, LANES), 1)
    picked = lane == first + lax.broadcasted_iota(jnp.int32, (slice_rows, LANES), 0)
    row = first + lax.broadcasted_iota(jnp.int32, (slice_rows, 1), 0)
    square = lax.broadcasted_iota(jnp.int32, (slice_rows, slice_rows), 0)
    square = square == lax.broadcasted_iota(jnp.int32, (slice_rows, slice_rows), 1)
    tiles = [in_ref[i, tail:lines, :].astype(jnp.float32) for i in range(pair_count)]
    for local in range(2):
        at = 3 * local
        logs = [
            tile[at : at + 1, :] + tile[at + 1 : at + 2, :] + tile[at + 2 : at + 3, :]
            for tile in tiles
        ]
        top = logs[0]
        for one in logs[1:]:
            top = jnp.maximum(top, one)
        scales = [jnp.exp(one - top) for one in logs]
        mass = scales[0]
        for one in scales[1:]:
            mass = mass + one
        share = 1.0 / mass
        columns = [
            jnp.sum(jnp.where(picked, scale * share, 0.0), axis=1, keepdims=True)
            for scale in scales
        ]
        valid = row < counts_ref[2 * lax.axis_index("own") + local]
        for i in range(features // LANES):
            there = (2 * i + local) * slice_rows
            here = slice(there, there + slice_rows)
            near = columns[0] * in_ref[0, here, :].astype(jnp.float32)
            for j in range(1, pair_count):
                near = near + columns[j] * in_ref[j, here, :].astype(jnp.float32)
            near_ref[local, :, i * LANES : (i + 1) * LANES] = jnp.where(valid, near, 0.0).astype(
                near_ref.dtype
            )
        column = jnp.sum(jnp.where(picked, top + jnp.log(mass), 0.0), axis=1, keepdims=True)
        column = jnp.where(valid, column, 0.0)
        log_ref[local : local + 1, :] = jnp.sum(
            jnp.where(square, column, 0.0), axis=0, keepdims=True
        )


def merged(counts, arrived, rows, features):
    pair_count = arrived.shape[0]
    vmem = pl.BlockSpec(memory_space=pltpu.VMEM)
    return pl.pallas_call(
        merge_kernel,
        out_shape=(
            jax.ShapeDtypeStruct((2, rows, features), jnp.bfloat16),
            jax.ShapeDtypeStruct((2, rows), jnp.float32),
        ),
        in_specs=[pl.BlockSpec(memory_space=pltpu.SMEM), vmem],
        out_specs=(vmem, vmem),
        compiler_params=pltpu.CompilerParams(vmem_limit_bytes=16 << 20),
        cost_estimate=pl.CostEstimate(
            flops=8 * pair_count * rows * features,
            bytes_accessed=4 * (pair_count + 1) * rows * features,
            transcendentals=2 * pair_count * rows,
        ),
        name="merged",
    )(counts, arrived)


def body(embeddings, cluster_sizes, row_counts):
    block_rows = embeddings.shape[1]
    own_count, pair_count = lax.axis_size("own"), lax.axis_size("pair")
    part = block_rows // (pair_count // 2)

    own_part = first_part(embeddings, part)
    embeddings, own_part = lax.optimization_barrier((embeddings, own_part))
    shards = {by: handed_on(own_part, by, own_count, pair_count) for by in (3, 1)}
    shards[6] = handed_on(shards[3][:part], 3, own_count, pair_count)
    shards[5] = handed_on(shards[3], 2, own_count, pair_count)
    both = jnp.concatenate([shards[1], shards[3]])
    shards[4] = handed_on(both, 1, own_count, pair_count)
    near = near_states(
        cluster_sizes, row_counts, embeddings, [own_part] + [shards[by] for by in (1, 3)]
    )
    states = all_states(near, [shards[by] for by in (5, 4, 6)], pair_count)
    arrived = lax.all_to_all(states, "pair", split_axis=0, concat_axis=0, tiled=True)
    return merged(row_counts, arrived, block_rows // pair_count, embeddings.shape[2])


def solution(mesh):
    placed = (P("own", None, None), P(), P())
    return jax.shard_map(
        body,
        mesh=mesh,
        in_specs=placed,
        out_specs=(P("own", "pair", None), P("own", "pair")),
        check_vma=False,
    )
```

```python
import jax
import jax.numpy as jnp
from jax import lax
from jax.experimental import pallas as pl
from jax.experimental.pallas import tpu as pltpu
from jax.sharding import PartitionSpec as P

SHARPNESS = 128.0
NEGATIVE = -1e30
NEAR = ((0, 0), (0, 1), (1, 0), (1, 1), (3, 0), (3, 1))
FAR = ((5, 0), (5, 1), (2, 0), (2, 1), (4, 0), (4, 1), (6, 0))
LANES = 128
STATS = 8
AXES = ("own", "pair")


def handed_on(shard, by, own_count, pair_count):
    pairs = []
    for owner in range(own_count):
        for place in range(pair_count):
            target = owner + (by if place % 2 == 0 else -by)
            if 0 <= target < own_count:
                pairs.append((owner * pair_count + place, target * pair_count + place))
    return lax.ppermute(shard, AXES, pairs)


def unit_rows(values):
    squares = jnp.sum(values * values, axis=-1, keepdims=True)
    return (values * lax.rsqrt(squares + 1e-06)).astype(jnp.bfloat16)


def part_kernel(x_ref, part_ref, rows, sems):
    part = rows.shape[1]
    place = lax.axis_index("pair")
    side = lax.rem(place, 2)
    start = pl.multiple_of(lax.shift_right_logical(place, 1) * part, part)
    copies = []
    for half in range(2):
        copies.append(
            pltpu.make_async_copy(
                x_ref.at[side if half else 1 - side, pl.ds(start, part), :], rows.at[half], sems.at[half]
            )
        )
        copies[half].start()
    for half in range(2):
        copies[half].wait()
        part_ref[half * part : (half + 1) * part, :] = unit_rows(rows[half])


def first_part(embeddings, part):
    features = embeddings.shape[2]
    return pl.pallas_call(
        part_kernel,
        out_shape=jax.ShapeDtypeStruct((2 * part, features), jnp.bfloat16),
        in_specs=[pl.BlockSpec(memory_space=pltpu.HBM)],
        out_specs=pl.BlockSpec(memory_space=pltpu.VMEM),
        scratch_shapes=[
            pltpu.VMEM((2, part, features), jnp.float32),
            pltpu.SemaphoreType.DMA((2,)),
        ],
        compiler_params=pltpu.CompilerParams(vmem_limit_bytes=4 << 20),
        cost_estimate=pl.CostEstimate(
            flops=8 * part * features, bytes_accessed=12 * part * features, transcendentals=2 * part
        ),
        name="first_part",
    )(pltpu.with_memory_space_constraint(embeddings, pltpu.HBM))


def key_tables(sizes_ref, counts_ref, pieces, part):
    own, place = lax.axis_index("own"), lax.axis_index("pair")
    side = lax.rem(place, 2)
    block_total = counts_ref.shape[0]
    lanes = part * len(pieces)
    bounds = [[jnp.int32(0), jnp.int32(0)] for local in range(2)]
    start = jnp.int32(0)
    for c in range(sizes_ref.shape[0]):
        end = start + sizes_ref[c]
        for local in range(2):
            block = 2 * own + local
            inside = (start <= block) & (block < end)
            bounds[local][0] = jnp.where(inside, start, bounds[local][0])
            bounds[local][1] = jnp.where(inside, end, bounds[local][1])
        start = end
    lane = lax.broadcasted_iota(jnp.int32, (1, lanes), 1)
    piece = lane // part
    sub = lane % part
    row = lax.shift_right_logical(place, 1) * part + sub
    count = jnp.zeros((1, lanes), jnp.int32)
    blocks = jnp.full((1, lanes), -1, jnp.int32)
    for i, (offset, half) in enumerate(pieces):
        block = 2 * (own + jnp.where(side == 0, -offset, offset)) + (side if half else 1 - side)
        there = (block >= 0) & (block < block_total)
        valid = counts_ref[jnp.clip(block, 0, block_total - 1)]
        here = piece == i
        count = jnp.where(here, jnp.where(there, valid, 0), count)
        blocks = jnp.where(here, block, blocks)
    usable = row < count
    if pieces[0][0] == 0:
        usable = usable & ((lane >= 2 * part) | (sub // (part // 2) == side))
    linked = [
        jnp.where(usable & (blocks >= low) & (blocks < high), 1, 0) for low, high in bounds
    ]
    return blocks * (4 * part) + row, linked


def attend(queries, keys, kept):
    scores = SHARPNESS * lax.dot_general(
        queries, keys, (((1,), (1,)), ((), ())), preferred_element_type=jnp.float32
    )
    scores = jnp.where(kept, scores, NEGATIVE)
    top = jnp.max(scores, axis=1, keepdims=True)
    weight = jnp.where(kept, jnp.exp(scores - top), 0.0)
    mass = jnp.sum(weight, axis=1, keepdims=True)
    total = jnp.dot(weight.astype(jnp.bfloat16), keys, preferred_element_type=jnp.float32)
    return top, mass, total


def gathered(keys, refs):
    start = 0
    for ref in refs:
        keys[start : start + ref.shape[0], :] = ref[...]
        start += ref.shape[0]


def near_kernel(sizes_ref, counts_ref, x_ref, *refs):
    *key_refs, q_ref, total_ref, state_ref, far_ref, keys = refs
    part = key_refs[0].shape[0] // 2
    block_rows = x_ref.shape[1]
    rows = q_ref.shape[0]
    for local in range(2):
        q_ref[local * block_rows : (local + 1) * block_rows, :] = unit_rows(x_ref[local])
    gathered(keys, key_refs)
    key_row, linked = key_tables(sizes_ref, counts_ref, NEAR, part)
    far = key_tables(sizes_ref, counts_ref, FAR, part)[1]
    for local in range(2):
        far_ref[local : local + 1, :] = far[local]
    query = lax.broadcasted_iota(jnp.int32, (rows, 1), 0)
    kept = jnp.where(query < block_rows, linked[0], linked[1]) != 0
    kept = kept & (key_row != lax.axis_index("own") * rows + query)
    top, mass, total = attend(q_ref[...], keys[...], kept)
    total_ref[...] = total
    lane = lax.broadcasted_iota(jnp.int32, (rows, LANES), 1)
    first_block = 2 * lax.axis_index("own")
    count = jnp.where(query < block_rows, counts_ref[first_block], counts_ref[first_block + 1])
    row = jnp.where(query < block_rows, query, query - block_rows)
    state_ref[...] = jnp.where(
        lane == 0, top, jnp.where(lane == 1, mass, jnp.where(row < count, 1.0, 0.0))
    )


def near_states(cluster_sizes, row_counts, embeddings, near_keys):
    _, block_rows, features = embeddings.shape
    rows = 2 * block_rows
    part = near_keys[0].shape[0] // 2
    key_rows = part * len(NEAR)
    far_rows = part * len(FAR)
    smem, vmem = (pl.BlockSpec(memory_space=m) for m in (pltpu.SMEM, pltpu.VMEM))
    return pl.pallas_call(
        near_kernel,
        out_shape=(
            jax.ShapeDtypeStruct((rows, features), jnp.bfloat16),
            jax.ShapeDtypeStruct((rows, features), jnp.float32),
            jax.ShapeDtypeStruct((rows, LANES), jnp.float32),
            jax.ShapeDtypeStruct((2, far_rows), jnp.int32),
        ),
        in_specs=[smem, smem] + [vmem] * (1 + len(near_keys)),
        out_specs=(vmem,) * 4,
        scratch_shapes=[pltpu.VMEM((key_rows, features), jnp.bfloat16)],
        compiler_params=pltpu.CompilerParams(vmem_limit_bytes=24 << 20),
        cost_estimate=pl.CostEstimate(
            flops=4 * rows * key_rows * features,
            bytes_accessed=10 * rows * features,
            transcendentals=rows * key_rows,
        ),
        name="near_states",
    )(cluster_sizes, row_counts, embeddings, *near_keys)


def far_kernel(q_ref, total_ref, state_ref, far_ref, *refs):
    *key_refs, out_ref, keys = refs
    gathered(keys, key_refs)
    rows, features = q_ref.shape
    block_rows = rows // 2
    pair_count = out_ref.shape[0]
    slice_rows = block_rows // pair_count
    query = lax.broadcasted_iota(jnp.int32, (rows, 1), 0)
    kept = jnp.where(query < block_rows, far_ref[0:1, :], far_ref[1:2, :]) != 0
    far_top, far_mass, far_total = attend(q_ref[...], keys[...], kept)
    near_top, near_mass = state_ref[:, 0:1], state_ref[:, 1:2]
    top = jnp.maximum(near_top, far_top)
    near_scale, far_scale = jnp.exp(near_top - top), jnp.exp(far_top - top)
    mass = near_scale * near_mass + far_scale * far_mass
    some = mass > 0.0
    safe = jnp.where(some, mass, 1.0)
    wanted = some & (state_ref[:, 2:3] > 0.0)
    near_scale, far_scale = near_scale / safe, far_scale / safe
    log_mass = jnp.where(wanted, top + jnp.log(safe), NEGATIVE)
    mean = (near_scale * total_ref[...] + far_scale * far_total).astype(jnp.bfloat16)
    across = lax.broadcasted_iota(jnp.int32, (block_rows, block_rows), 0)
    across = across == lax.broadcasted_iota(jnp.int32, (block_rows, block_rows), 1)
    line = lax.broadcasted_iota(jnp.int32, (STATS, block_rows), 0)
    pieces = jnp.zeros((STATS, block_rows), jnp.float32)
    for local in range(2):
        column = log_mass[local * block_rows : (local + 1) * block_rows, :]
        logs = jnp.sum(jnp.where(across, column, 0.0), axis=0, keepdims=True)
        high = logs.astype(jnp.bfloat16).astype(jnp.float32)
        middle = (logs - high).astype(jnp.bfloat16).astype(jnp.float32)
        for i, piece in enumerate((high, middle, logs - high - middle)):
            pieces = jnp.where(line == 3 * local + i, piece, pieces)
    pieces = pieces.astype(jnp.bfloat16)
    for place in range(pair_count):
        for local in range(2):
            first = local * block_rows + place * slice_rows
            for i in range(features // LANES):
                there = (2 * i + local) * slice_rows
                out_ref[place, there : there + slice_rows, :] = mean[
                    first : first + slice_rows, i * LANES : (i + 1) * LANES
                ]
        tail = 2 * slice_rows * (features // LANES)
        out_ref[place, tail : tail + STATS, :] = pieces


def all_states(near, far_keys, pair_count):
    rows, features = near[0].shape
    key_rows = sum(keys.shape[0] for keys in far_keys)
    vmem = pl.BlockSpec(memory_space=pltpu.VMEM)
    return pl.pallas_call(
        far_kernel,
        out_shape=jax.ShapeDtypeStruct(
            (pair_count, rows // pair_count * (features // LANES) + STATS, LANES), jnp.bfloat16
        ),
        in_specs=[vmem] * (len(near) + len(far_keys)),
        out_specs=vmem,
        scratch_shapes=[pltpu.VMEM((key_rows, features), jnp.bfloat16)],
        compiler_params=pltpu.CompilerParams(vmem_limit_bytes=24 << 20),
        cost_estimate=pl.CostEstimate(
            flops=4 * rows * key_rows * features,
            bytes_accessed=8 * rows * features,
            transcendentals=rows * key_rows,
        ),
        name="all_states",
    )(*near, *far_keys)


def merge_kernel(in_ref, near_ref, log_ref):
    pair_count, lines, _ = in_ref.shape
    slice_rows, features = near_ref.shape[1:]
    tail = lines - STATS
    place = lax.axis_index("pair")
    first = place * slice_rows
    lane = lax.broadcasted_iota(jnp.int32, (slice_rows, LANES), 1)
    picked = lane == first + lax.broadcasted_iota(jnp.int32, (slice_rows, LANES), 0)
    square = lax.broadcasted_iota(jnp.int32, (slice_rows, slice_rows), 0)
    square = square == lax.broadcasted_iota(jnp.int32, (slice_rows, slice_rows), 1)
    tiles = [in_ref[i, tail:lines, :].astype(jnp.float32) for i in range(pair_count)]
    for local in range(2):
        at = 3 * local
        logs = [
            tile[at : at + 1, :] + tile[at + 1 : at + 2, :] + tile[at + 2 : at + 3, :]
            for tile in tiles
        ]
        top = logs[0]
        for one in logs[1:]:
            top = jnp.maximum(top, one)
        scales = [jnp.exp(one - top) for one in logs]
        mass = scales[0]
        for one in scales[1:]:
            mass = mass + one
        valid = top > 0.5 * NEGATIVE
        share = jnp.where(valid, 1.0 / mass, 0.0)
        columns = [
            jnp.sum(jnp.where(picked, scale * share, 0.0), axis=1, keepdims=True)
            for scale in scales
        ]
        for i in range(features // LANES):
            there = (2 * i + local) * slice_rows
            here = slice(there, there + slice_rows)
            near = columns[0] * in_ref[0, here, :].astype(jnp.float32)
            for j in range(1, pair_count):
                near = near + columns[j] * in_ref[j, here, :].astype(jnp.float32)
            near_ref[local, :, i * LANES : (i + 1) * LANES] = near.astype(near_ref.dtype)
        logs = jnp.where(valid, top + jnp.log(mass), 0.0)
        column = jnp.sum(jnp.where(picked, logs, 0.0), axis=1, keepdims=True)
        log_ref[local : local + 1, :] = jnp.sum(
            jnp.where(square, column, 0.0), axis=0, keepdims=True
        )


def merged(arrived, rows, features):
    pair_count = arrived.shape[0]
    vmem = pl.BlockSpec(memory_space=pltpu.VMEM)
    return pl.pallas_call(
        merge_kernel,
        out_shape=(
            jax.ShapeDtypeStruct((2, rows, features), jnp.bfloat16),
            jax.ShapeDtypeStruct((2, rows), jnp.float32),
        ),
        in_specs=[vmem],
        out_specs=(vmem, vmem),
        compiler_params=pltpu.CompilerParams(vmem_limit_bytes=16 << 20),
        cost_estimate=pl.CostEstimate(
            flops=8 * pair_count * rows * features,
            bytes_accessed=4 * (pair_count + 1) * rows * features,
            transcendentals=2 * pair_count * rows,
        ),
        name="merged",
    )(arrived)


def body(embeddings, cluster_sizes, row_counts):
    block_rows = embeddings.shape[1]
    own_count, pair_count = lax.axis_size("own"), lax.axis_size("pair")
    part = block_rows // (pair_count // 2)

    own_part = first_part(embeddings, part)
    embeddings, own_part = lax.optimization_barrier((embeddings, own_part))
    shards = {by: handed_on(own_part, by, own_count, pair_count) for by in (3, 1)}
    shards[6] = handed_on(shards[3][:part], 3, own_count, pair_count)
    shards[5] = handed_on(shards[3], 2, own_count, pair_count)
    both = jnp.concatenate([shards[1], shards[3]])
    shards[4] = handed_on(both, 1, own_count, pair_count)
    near = near_states(
        cluster_sizes, row_counts, embeddings, [own_part] + [shards[by] for by in (1, 3)]
    )
    states = all_states(near, [shards[by] for by in (5, 4, 6)], pair_count)
    arrived = lax.all_to_all(states, "pair", split_axis=0, concat_axis=0, tiled=True)
    return merged(arrived, block_rows // pair_count, embeddings.shape[2])


def solution(mesh):
    placed = (P("own", None, None), P(), P())
    return jax.shard_map(
        body,
        mesh=mesh,
        in_specs=placed,
        out_specs=(P("own", "pair", None), P("own", "pair")),
        check_vma=False,
    )
```

```python
import jax
import jax.numpy as jnp
from jax import lax
from jax.experimental import pallas as pl
from jax.experimental.pallas import tpu as pltpu
from jax.sharding import PartitionSpec as P

SHARPNESS = 128.0
NEGATIVE = -1e30
NEAR = ((0, 0), (0, 1), (1, 0), (1, 1), (3, 0), (3, 1))
FAR = ((5, 0), (5, 1), (2, 0), (2, 1), (4, 0), (4, 1), (6, 0))
LANES = 128
STATS = 8
AXES = ("own", "pair")


def handed_on(shard, by, own_count, pair_count):
    pairs = []
    for owner in range(own_count):
        for place in range(pair_count):
            target = owner + (by if place % 2 == 0 else -by)
            if 0 <= target < own_count:
                pairs.append((owner * pair_count + place, target * pair_count + place))
    return lax.ppermute(shard, AXES, pairs)


def unit_rows(values):
    squares = jnp.sum(values * values, axis=-1, keepdims=True)
    return (values * lax.rsqrt(squares + 1e-06)).astype(jnp.bfloat16)


def part_kernel(x_ref, part_ref, rows, sems):
    part = rows.shape[1]
    place = lax.axis_index("pair")
    side = lax.rem(place, 2)
    start = pl.multiple_of(lax.shift_right_logical(place, 1) * part, part)
    copies = []
    for half in range(2):
        copies.append(
            pltpu.make_async_copy(
                x_ref.at[side if half else 1 - side, pl.ds(start, part), :], rows.at[half], sems.at[half]
            )
        )
        copies[half].start()
    for half in range(2):
        copies[half].wait()
        part_ref[half * part : (half + 1) * part, :] = unit_rows(rows[half])


def first_part(embeddings, part):
    features = embeddings.shape[2]
    return pl.pallas_call(
        part_kernel,
        out_shape=jax.ShapeDtypeStruct((2 * part, features), jnp.bfloat16),
        in_specs=[pl.BlockSpec(memory_space=pltpu.HBM)],
        out_specs=pl.BlockSpec(memory_space=pltpu.VMEM),
        scratch_shapes=[
            pltpu.VMEM((2, part, features), jnp.float32),
            pltpu.SemaphoreType.DMA((2,)),
        ],
        compiler_params=pltpu.CompilerParams(vmem_limit_bytes=4 << 20),
        cost_estimate=pl.CostEstimate(
            flops=8 * part * features, bytes_accessed=12 * part * features, transcendentals=2 * part
        ),
        name="first_part",
    )(pltpu.with_memory_space_constraint(embeddings, pltpu.HBM))


def key_tables(sizes_ref, counts_ref, pieces, part):
    own, place = lax.axis_index("own"), lax.axis_index("pair")
    side = lax.rem(place, 2)
    block_total = counts_ref.shape[0]
    lanes = part * len(pieces)
    bounds = [[jnp.int32(0), jnp.int32(0)] for local in range(2)]
    start = jnp.int32(0)
    for c in range(sizes_ref.shape[0]):
        end = start + sizes_ref[c]
        for local in range(2):
            block = 2 * own + local
            inside = (start <= block) & (block < end)
            bounds[local][0] = jnp.where(inside, start, bounds[local][0])
            bounds[local][1] = jnp.where(inside, end, bounds[local][1])
        start = end
    lane = lax.broadcasted_iota(jnp.int32, (1, lanes), 1)
    piece = lane // part
    sub = lane % part
    row = lax.shift_right_logical(place, 1) * part + sub
    count = jnp.zeros((1, lanes), jnp.int32)
    blocks = jnp.full((1, lanes), -1, jnp.int32)
    for i, (offset, half) in enumerate(pieces):
        block = 2 * (own + jnp.where(side == 0, -offset, offset)) + (side if half else 1 - side)
        there = (block >= 0) & (block < block_total)
        valid = counts_ref[jnp.clip(block, 0, block_total - 1)]
        here = piece == i
        count = jnp.where(here, jnp.where(there, valid, 0), count)
        blocks = jnp.where(here, block, blocks)
    usable = row < count
    if pieces[0][0] == 0:
        usable = usable & ((lane >= 2 * part) | (sub // (part // 2) == side))
    linked = [
        jnp.where(usable & (blocks >= low) & (blocks < high), 1, 0) for low, high in bounds
    ]
    return blocks * (4 * part) + row, linked


def attend(queries, keys, kept):
    scores = SHARPNESS * lax.dot_general(
        queries, keys, (((1,), (1,)), ((), ())), preferred_element_type=jnp.float32
    )
    scores = jnp.where(kept, scores, NEGATIVE)
    top = jnp.max(scores, axis=1, keepdims=True)
    weight = jnp.where(kept, jnp.exp(scores - top), 0.0)
    mass = jnp.sum(weight, axis=1, keepdims=True)
    total = jnp.dot(weight.astype(jnp.bfloat16), keys, preferred_element_type=jnp.float32)
    return top, mass, total


def gathered(keys, refs):
    start = 0
    for ref in refs:
        keys[start : start + ref.shape[0], :] = ref[...]
        start += ref.shape[0]


def near_kernel(sizes_ref, counts_ref, x_ref, *refs):
    *key_refs, q_ref, total_ref, state_ref, far_ref, keys, held, sem = refs
    read = pltpu.make_async_copy(x_ref, held, sem)
    read.start()
    part = key_refs[0].shape[0] // 2
    block_rows = x_ref.shape[1]
    rows = q_ref.shape[0]
    gathered(keys, key_refs)
    key_row, linked = key_tables(sizes_ref, counts_ref, NEAR, part)
    far = key_tables(sizes_ref, counts_ref, FAR, part)[1]
    for local in range(2):
        far_ref[local : local + 1, :] = far[local]
    read.wait()
    for local in range(2):
        q_ref[local * block_rows : (local + 1) * block_rows, :] = unit_rows(held[local])
    query = lax.broadcasted_iota(jnp.int32, (rows, 1), 0)
    kept = jnp.where(query < block_rows, linked[0], linked[1]) != 0
    kept = kept & (key_row != lax.axis_index("own") * rows + query)
    top, mass, total = attend(q_ref[...], keys[...], kept)
    total_ref[...] = total
    lane = lax.broadcasted_iota(jnp.int32, (rows, LANES), 1)
    first_block = 2 * lax.axis_index("own")
    count = jnp.where(query < block_rows, counts_ref[first_block], counts_ref[first_block + 1])
    row = jnp.where(query < block_rows, query, query - block_rows)
    state_ref[...] = jnp.where(
        lane == 0, top, jnp.where(lane == 1, mass, jnp.where(row < count, 1.0, 0.0))
    )


def near_states(cluster_sizes, row_counts, embeddings, near_keys):
    _, block_rows, features = embeddings.shape
    rows = 2 * block_rows
    part = near_keys[0].shape[0] // 2
    key_rows = part * len(NEAR)
    far_rows = part * len(FAR)
    smem, vmem = (pl.BlockSpec(memory_space=m) for m in (pltpu.SMEM, pltpu.VMEM))
    return pl.pallas_call(
        near_kernel,
        out_shape=(
            jax.ShapeDtypeStruct((rows, features), jnp.bfloat16),
            jax.ShapeDtypeStruct((rows, features), jnp.float32),
            jax.ShapeDtypeStruct((rows, LANES), jnp.float32),
            jax.ShapeDtypeStruct((2, far_rows), jnp.int32),
        ),
        in_specs=[smem, smem, pl.BlockSpec(memory_space=pltpu.HBM)] + [vmem] * len(near_keys),
        out_specs=(vmem,) * 4,
        scratch_shapes=[
            pltpu.VMEM((key_rows, features), jnp.bfloat16),
            pltpu.VMEM(embeddings.shape, jnp.float32),
            pltpu.SemaphoreType.DMA,
        ],
        compiler_params=pltpu.CompilerParams(vmem_limit_bytes=24 << 20),
        cost_estimate=pl.CostEstimate(
            flops=4 * rows * key_rows * features,
            bytes_accessed=10 * rows * features,
            transcendentals=rows * key_rows,
        ),
        name="near_states",
    )(
        cluster_sizes,
        row_counts,
        pltpu.with_memory_space_constraint(embeddings, pltpu.HBM),
        *near_keys,
    )


def far_kernel(q_ref, total_ref, state_ref, far_ref, *refs):
    *key_refs, out_ref, keys = refs
    gathered(keys, key_refs)
    rows, features = q_ref.shape
    block_rows = rows // 2
    pair_count = out_ref.shape[0]
    slice_rows = block_rows // pair_count
    query = lax.broadcasted_iota(jnp.int32, (rows, 1), 0)
    kept = jnp.where(query < block_rows, far_ref[0:1, :], far_ref[1:2, :]) != 0
    far_top, far_mass, far_total = attend(q_ref[...], keys[...], kept)
    near_top, near_mass = state_ref[:, 0:1], state_ref[:, 1:2]
    top = jnp.maximum(near_top, far_top)
    near_scale, far_scale = jnp.exp(near_top - top), jnp.exp(far_top - top)
    mass = near_scale * near_mass + far_scale * far_mass
    some = mass > 0.0
    safe = jnp.where(some, mass, 1.0)
    wanted = some & (state_ref[:, 2:3] > 0.0)
    near_scale, far_scale = near_scale / safe, far_scale / safe
    log_mass = jnp.where(wanted, top + jnp.log(safe), NEGATIVE)
    mean = (near_scale * total_ref[...] + far_scale * far_total).astype(jnp.bfloat16)
    across = lax.broadcasted_iota(jnp.int32, (block_rows, block_rows), 0)
    across = across == lax.broadcasted_iota(jnp.int32, (block_rows, block_rows), 1)
    line = lax.broadcasted_iota(jnp.int32, (STATS, block_rows), 0)
    pieces = jnp.zeros((STATS, block_rows), jnp.float32)
    for local in range(2):
        column = log_mass[local * block_rows : (local + 1) * block_rows, :]
        logs = jnp.sum(jnp.where(across, column, 0.0), axis=0, keepdims=True)
        high = logs.astype(jnp.bfloat16).astype(jnp.float32)
        middle = (logs - high).astype(jnp.bfloat16).astype(jnp.float32)
        for i, piece in enumerate((high, middle, logs - high - middle)):
            pieces = jnp.where(line == 3 * local + i, piece, pieces)
    pieces = pieces.astype(jnp.bfloat16)
    for place in range(pair_count):
        for local in range(2):
            first = local * block_rows + place * slice_rows
            for i in range(features // LANES):
                there = (2 * i + local) * slice_rows
                out_ref[place, there : there + slice_rows, :] = mean[
                    first : first + slice_rows, i * LANES : (i + 1) * LANES
                ]
        tail = 2 * slice_rows * (features // LANES)
        out_ref[place, tail : tail + STATS, :] = pieces


def all_states(near, far_keys, pair_count):
    rows, features = near[0].shape
    key_rows = sum(keys.shape[0] for keys in far_keys)
    vmem = pl.BlockSpec(memory_space=pltpu.VMEM)
    return pl.pallas_call(
        far_kernel,
        out_shape=jax.ShapeDtypeStruct(
            (pair_count, rows // pair_count * (features // LANES) + STATS, LANES), jnp.bfloat16
        ),
        in_specs=[vmem] * (len(near) + len(far_keys)),
        out_specs=vmem,
        scratch_shapes=[pltpu.VMEM((key_rows, features), jnp.bfloat16)],
        compiler_params=pltpu.CompilerParams(vmem_limit_bytes=24 << 20),
        cost_estimate=pl.CostEstimate(
            flops=4 * rows * key_rows * features,
            bytes_accessed=8 * rows * features,
            transcendentals=rows * key_rows,
        ),
        name="all_states",
    )(*near, *far_keys)


def merge_kernel(in_ref, near_ref, log_ref):
    pair_count, lines, _ = in_ref.shape
    slice_rows, features = near_ref.shape[1:]
    tail = lines - STATS
    place = lax.axis_index("pair")
    first = place * slice_rows
    lane = lax.broadcasted_iota(jnp.int32, (slice_rows, LANES), 1)
    picked = lane == first + lax.broadcasted_iota(jnp.int32, (slice_rows, LANES), 0)
    square = lax.broadcasted_iota(jnp.int32, (slice_rows, slice_rows), 0)
    square = square == lax.broadcasted_iota(jnp.int32, (slice_rows, slice_rows), 1)
    tiles = [in_ref[i, tail:lines, :].astype(jnp.float32) for i in range(pair_count)]
    for local in range(2):
        at = 3 * local
        logs = [
            tile[at : at + 1, :] + tile[at + 1 : at + 2, :] + tile[at + 2 : at + 3, :]
            for tile in tiles
        ]
        top = logs[0]
        for one in logs[1:]:
            top = jnp.maximum(top, one)
        scales = [jnp.exp(one - top) for one in logs]
        mass = scales[0]
        for one in scales[1:]:
            mass = mass + one
        valid = top > 0.5 * NEGATIVE
        share = jnp.where(valid, 1.0 / mass, 0.0)
        columns = [
            jnp.sum(jnp.where(picked, scale * share, 0.0), axis=1, keepdims=True)
            for scale in scales
        ]
        for i in range(features // LANES):
            there = (2 * i + local) * slice_rows
            here = slice(there, there + slice_rows)
            near = columns[0] * in_ref[0, here, :].astype(jnp.float32)
            for j in range(1, pair_count):
                near = near + columns[j] * in_ref[j, here, :].astype(jnp.float32)
            near_ref[local, :, i * LANES : (i + 1) * LANES] = near.astype(near_ref.dtype)
        logs = jnp.where(valid, top + jnp.log(mass), 0.0)
        column = jnp.sum(jnp.where(picked, logs, 0.0), axis=1, keepdims=True)
        log_ref[local : local + 1, :] = jnp.sum(
            jnp.where(square, column, 0.0), axis=0, keepdims=True
        )


def merged(arrived, rows, features):
    pair_count = arrived.shape[0]
    vmem = pl.BlockSpec(memory_space=pltpu.VMEM)
    return pl.pallas_call(
        merge_kernel,
        out_shape=(
            jax.ShapeDtypeStruct((2, rows, features), jnp.bfloat16),
            jax.ShapeDtypeStruct((2, rows), jnp.float32),
        ),
        in_specs=[vmem],
        out_specs=(vmem, vmem),
        compiler_params=pltpu.CompilerParams(vmem_limit_bytes=16 << 20),
        cost_estimate=pl.CostEstimate(
            flops=8 * pair_count * rows * features,
            bytes_accessed=4 * (pair_count + 1) * rows * features,
            transcendentals=2 * pair_count * rows,
        ),
        name="merged",
    )(arrived)


def body(embeddings, cluster_sizes, row_counts):
    block_rows = embeddings.shape[1]
    own_count, pair_count = lax.axis_size("own"), lax.axis_size("pair")
    part = block_rows // (pair_count // 2)

    own_part = first_part(embeddings, part)
    embeddings, own_part = lax.optimization_barrier((embeddings, own_part))
    shards = {by: handed_on(own_part, by, own_count, pair_count) for by in (3, 1)}
    shards[6] = handed_on(shards[3][:part], 3, own_count, pair_count)
    shards[5] = handed_on(shards[3], 2, own_count, pair_count)
    both = jnp.concatenate([shards[1], shards[3]])
    shards[4] = handed_on(both, 1, own_count, pair_count)
    near = near_states(
        cluster_sizes, row_counts, embeddings, [own_part] + [shards[by] for by in (1, 3)]
    )
    states = all_states(near, [shards[by] for by in (5, 4, 6)], pair_count)
    arrived = lax.all_to_all(states, "pair", split_axis=0, concat_axis=0, tiled=True)
    return merged(arrived, block_rows // pair_count, embeddings.shape[2])


def solution(mesh):
    placed = (P("own", None, None), P(), P())
    return jax.shard_map(
        body,
        mesh=mesh,
        in_specs=placed,
        out_specs=(P("own", "pair", None), P("own", "pair")),
        check_vma=False,
    )
```
